32 devices in a mesh: grp: 2 (over x), row: 16 (over z, y, core).
Axes of the slice: x: 2, y: 2, z: 4, core: 2. Of those that a mesh axis runs over, the one named last changes fastest.
Arguments:
- start: float32 [3, 262144], P(None, ('grp', 'row')), parts along dimension 1, may hold values from -6 to 6
- rhs: float32 [3, 262144], P(None, ('grp', 'row')), parts along dimension 1, may hold values from -6 to 6
- fine_vals: bfloat16 [3, 3, 12, 262144], P(None, None, None, ('grp', 'row')), parts along dimension 3
- fine_cols: int32 [12, 262144], P(None, ('grp', 'row')), parts along dimension 1, may hold values from 0 to 16383, as said below
- prol: bfloat16 [3, 3, 262144], P(None, None, ('grp', 'row')), parts along dimension 2, may hold values from -3 to 3
- aggregate: int32 [262144], P(('grp', 'row')), parts along dimension 0, may hold values from 0 to 8191, as said below
- coarse_vals: bfloat16 [3, 3, 12, 16384], P(None, None, None, ('grp', 'row')), parts along dimension 3
- coarse_cols: int32 [12, 16384], P(None, ('grp', 'row')), parts along dimension 1, may hold values from 0 to 1023, as said below
Outputs:
- fine_iterate: float32 [3, 262144], P(None, ('grp', 'row')), parts along dimension 1
- coarse_iterate: float32 [3, 16384], P(None, ('grp', 'row')), parts along dimension 1
- coarse_residual: float32 [3, 16384], P(None, ('grp', 'row')), parts along dimension 1
The draws below stay inside these ranges and needn't reach their ends.
There are 2 independent parts, one for each index of `grp`. The reference program is written for one: setup_inputs(seed, part) draws one part's arguments, and reference() takes and returns one part's arrays. A program takes and returns all parts, laid end to end along the dimension named above; each array names one. Nothing has to cross between parts.
Inputs may be any that keep to these rules, and one draw needn't show every extreme that they name: `fine_cols`: slot 0 of every row holds 4096 + the node's position on its device; every index is a position in a device's 8192 nodes extended by 4096 nodes of each neighbouring device on either side (position 0 is the first of the lower neighbour's last 4096 nodes). `coarse_cols`: slot 0 of every row holds 256 + the aggregate's position on its device; every index is a position in a device's 512 aggregates extended by 256 aggregates of each neighbouring device on either side. A fine node of device block d lies in an aggregate from 512 * d - 16 to 512 * (d + 1) + 15.
All inputs are finite; a program needn't handle non-finite values.
Results may differ from the reference program's by a relative error of at most 0.0003.
Values sent between devices are 32-bit elements; how exact they have to be, the bound alone decides.
A program may use at most 128 MiB of HBM per device.

```python
import jax
import jax.numpy as jnp
from jax import lax

LAYER = 4096
K = 12
KC = 12
RATIO = 16
NF = 8192
NC = 512
WIN = 16
NODES = 131072
CTOT = 8192


def block_values(noise, key, rows):
    position = jnp.arange(rows, dtype=jnp.float32) / rows
    growth = 1.0 + 2.0 * position
    values = 0.05 * noise * growth
    diagonal = jax.random.uniform(key, (3, rows), jnp.float32, 1.5, 3.0)
    for comp in range(3):
        values = values.at[comp, comp, 0].set(diagonal[comp])
    return values.astype(jnp.bfloat16)


def stencil_columns(key, kk, rows, block, layer):
    key_shift, key_jitter = jax.random.split(key)
    local = jnp.arange(rows, dtype=jnp.int32) % block
    reach = max(layer // 16, 1)
    shift = jax.random.randint(key_shift, (kk, rows), -1, 2, dtype=jnp.int32)
    jitter = jax.random.randint(key_jitter, (kk, rows), -reach, reach + 1, dtype=jnp.int32)
    columns = layer + local[None, :] + shift * layer + jitter
    columns = jnp.clip(columns, 0, block + 2 * layer - 1)
    columns = columns.at[0].set(layer + local)
    return columns.astype(jnp.int32)


def draw_fine_vals(key, part):
    key_noise, key_diag = jax.random.split(jax.random.fold_in(key, 11))
    noise = jax.random.normal(key_noise, (3, 3, K, NODES), jnp.float32)
    return block_values(noise, key_diag, NODES)


def draw_coarse_vals(key, part):
    key_noise, key_diag = jax.random.split(jax.random.fold_in(key, 13))
    noise = jax.random.normal(key_noise, (3, 3, KC, CTOT), jnp.float32)
    return block_values(noise, key_diag, CTOT)


def draw_fine_cols(key, part):
    return stencil_columns(jax.random.fold_in(key, 17), K, NODES, NF, LAYER)


def draw_coarse_cols(key, part):
    return stencil_columns(jax.random.fold_in(key, 19), KC, CTOT, NC, NC // 2)


def draw_aggregate(key, part):
    index = jnp.arange(NODES, dtype=jnp.int32)
    device = index // NF
    local = index % NF
    jitter = jax.random.randint(jax.random.fold_in(key, 23), (NODES,), -WIN, WIN + 1, dtype=jnp.int32)
    jitter = jnp.where(local == 0, -WIN, jnp.where(local == NF - 1, WIN, jitter))
    owner = device * NC + local // RATIO + jitter
    return jnp.clip(owner, 0, CTOT - 1).astype(jnp.int32)


def level_of(stream_key, shape, shards, low, largest):
    gain, own = 1.0, jax.random.fold_in(stream_key, 6)
    for dim, shards_of in shards:
        steps = jnp.exp(jax.random.uniform(jax.random.fold_in(own, dim), (shards_of,), jnp.float32, low / len(shards), largest / len(shards)))
        gain = gain * jnp.repeat(steps, shape[dim] // shards_of).reshape([-1 if axis == dim else 1 for axis in range(len(shape))])
    return gain


def scatter_about(key, dims, spread, limit, cuts=(), held_as=jnp.bfloat16):
    values = spread * jax.random.normal(key, dims, jnp.float32)
    if cuts:
        values = values * level_of(key, dims, cuts, -0.22, 0.18)
    return jnp.clip(values, -limit, limit).astype(held_as)


def setup_inputs(seed: int = 0, part: int = 0) -> dict:
    splits = jax.random.split(jax.random.key(seed), 9)
    part_keys = jax.random.split(jax.random.fold_in(splits[8], part), 9)
    return {
        "start": scatter_about(part_keys[0], (3, NODES), 1.0, 6.0, ((1, 16),), jnp.float32),
        "rhs": scatter_about(part_keys[1], (3, NODES), 1.0, 6.0, ((1, 16),), jnp.float32),
        "fine_vals": draw_fine_vals(jax.random.fold_in(jax.random.fold_in(splits[8], part), 71), part),
        "fine_cols": draw_fine_cols(jax.random.fold_in(jax.random.fold_in(splits[8], part), 71), part),
        "prol": scatter_about(part_keys[4], (3, 3, NODES), 0.5, 3.0, ((2, 16),)),
        "aggregate": draw_aggregate(jax.random.fold_in(jax.random.fold_in(splits[8], part), 71), part),
        "coarse_vals": draw_coarse_vals(jax.random.fold_in(jax.random.fold_in(splits[8], part), 71), part),
        "coarse_cols": draw_coarse_cols(jax.random.fold_in(jax.random.fold_in(splits[8], part), 71), part),
    }


lower_fraction = 0.1


def local_apply(extended, values, columns):
    gathered = extended[:, columns]
    return jnp.sum(values.astype(jnp.float32) * gathered[None], axis=(1, 2))


def apply_global(vector, values, columns, block, width):
    blocks = vector.shape[1] // block
    padded = jnp.pad(vector, ((0, 0), (width, width)))
    zero = jnp.int32(0)

    def one_block(index):
        first = index * jnp.int32(block)
        extended = lax.dynamic_slice(padded, (zero, first), (3, block + 2 * width))
        part_vals = lax.dynamic_slice(values, (zero, zero, zero, first), (3, 3, values.shape[2], block))
        part_cols = lax.dynamic_slice(columns, (zero, first), (columns.shape[0], block))
        return local_apply(extended, part_vals, part_cols)

    result = lax.map(one_block, jnp.arange(blocks, dtype=jnp.int32))
    return jnp.transpose(result, (1, 0, 2)).reshape(3, -1)


def diag_inverse(values):
    return 1.0 / jnp.stack([values[c, c, 0] for c in range(3)]).astype(jnp.float32)


def spectral_bound(values, inverse):
    return jnp.max(jnp.sum(jnp.abs(values.astype(jnp.float32)), axis=(1, 2)) * inverse)


def coefficients(bound):
    lowest = lower_fraction * bound
    theta = (bound + lowest) / 2.0
    delta = (bound - lowest) / 2.0
    sigma = theta / delta
    rho_zero = 1.0 / sigma
    rho_one = 1.0 / (2.0 * sigma - rho_zero)
    return theta, delta, rho_zero, rho_one


def chebyshev(operator, inverse, iterate, residual, bound):
    theta, delta, rho_zero, rho_one = coefficients(bound)
    first = inverse * residual / theta
    iterate = iterate + first
    residual = residual - operator(first)
    second = rho_one * rho_zero * first + (2.0 * rho_one / delta) * inverse * residual
    iterate = iterate + second
    residual = residual - operator(second)
    return iterate, residual


def reference(start, rhs, fine_vals, fine_cols, prol, aggregate, coarse_vals, coarse_cols):
    def fine_apply(vector):
        return apply_global(vector, fine_vals, fine_cols, NF, LAYER)

    def coarse_apply(vector):
        return apply_global(vector, coarse_vals, coarse_cols, NC, NC // 2)

    dinv = diag_inverse(fine_vals)
    bound = spectral_bound(fine_vals, dinv)
    cdinv = diag_inverse(coarse_vals)
    cbound = spectral_bound(coarse_vals, cdinv)
    residual = rhs - fine_apply(start)
    fine_iterate, fine_res = chebyshev(fine_apply, dinv, start, residual, bound)
    contrib = jnp.sum(prol.astype(jnp.float32) * fine_res[:, None, :], axis=0)
    restricted = jnp.zeros((3, CTOT), jnp.float32).at[:, aggregate].add(contrib)
    zeros = jnp.zeros((3, CTOT), jnp.float32)
    coarse_iterate, coarse_residual = chebyshev(coarse_apply, cdinv, zeros, restricted, cbound)
    return fine_iterate, coarse_iterate, coarse_residual
```

```python
import functools

import jax
import jax.numpy as jnp
from jax import lax
from jax.experimental import pallas as pl
from jax.experimental.pallas import tpu as pltpu
from jax.sharding import PartitionSpec as P

LANE = 128
CHUNK = 16
GROUP = 4
lower_fraction = 0.1

f32, i32, bf16 = jnp.float32, jnp.int32, jnp.bfloat16
VMEM = pl.BlockSpec(memory_space=pltpu.VMEM)
SMEM = pl.BlockSpec(memory_space=pltpu.SMEM)


def coefficients(bound):
    lowest = lower_fraction * bound
    theta = (bound + lowest) / 2.0
    delta = (bound - lowest) / 2.0
    sigma = theta / delta
    rho_zero = 1.0 / sigma
    rho_one = 1.0 / (2.0 * sigma - rho_zero)
    return (theta, delta, rho_zero, rho_one)


def at_block(b):
    if isinstance(b, int):
        return pl.ds(b * LANE, LANE)
    return pl.ds(pl.multiple_of(b * LANE, LANE), LANE)


def take_lanes(row, lanes):
    return jnp.take_along_axis(row, lanes, axis=1, mode="promise_in_bounds")


def pad_rows(x):
    return x[0:8], jnp.concatenate([x[8:12], x[8:12]], axis=0)


def halves(cols):
    parts = pad_rows(cols)
    return [p & (LANE - 1) for p in parts], [p >> 7 for p in parts]


def visit(table_ref, r, lanes, rows, acc):
    at = at_block(r)
    masks = [row == r for row in rows]
    out = []
    for j in range(3):
        src = jnp.broadcast_to(table_ref[j : j + 1, at], (8, LANE))
        for h in range(2):
            out.append(jnp.where(masks[h], take_lanes(src, lanes[h]), acc[2 * j + h]))
    return out


def contract(vals_ref, at, acc):
    out = []
    gathered = [jnp.concatenate([acc[2 * j], acc[2 * j + 1][0:4]], axis=0) for j in range(3)]
    for c in range(3):
        total = None
        for j in range(3):
            term = vals_ref[c, j, :, at].astype(f32) * gathered[j]
            total = term if total is None else total + term
        out.append(jnp.sum(total, axis=0, keepdims=True))
    return out


def bound_of_block(vals_ref, at, dinv_ref, best):
    for c in range(3):
        total = None
        for j in range(3):
            term = jnp.abs(vals_ref[c, j, :, at].astype(f32))
            total = term if total is None else total + term
        inverse = 1.0 / vals_ref[c, c, :, at].astype(f32)[0:1]
        dinv_ref[c : c + 1, at] = inverse
        best = jnp.maximum(best, jnp.sum(total, axis=0, keepdims=True) * inverse)
    return best


def neighbours(me, n):
    return ((me > 0, me - 1), (me < n - 1, me + 1))


def exchange(source, target, width, own, me, n, sends, recvs):
    low = pltpu.make_async_remote_copy(
        src_ref=source.at[:, pl.ds(0, width)],
        dst_ref=target.at[:, pl.ds(width + own, width)],
        send_sem=sends.at[0],
        recv_sem=recvs.at[0],
        device_id={"row": jnp.maximum(me - 1, 0)},
        device_id_type=pl.DeviceIdType.MESH,
    )
    high = pltpu.make_async_remote_copy(
        src_ref=source.at[:, pl.ds(own - width, width)],
        dst_ref=target.at[:, pl.ds(0, width)],
        send_sem=sends.at[1],
        recv_sem=recvs.at[1],
        device_id={"row": jnp.minimum(me + 1, n - 1)},
        device_id_type=pl.DeviceIdType.MESH,
    )

    def start():
        @pl.when(me > 0)
        def _():
            low.start()

        @pl.when(me < n - 1)
        def _():
            high.start()

        zeros = jnp.zeros((3, width), f32)

        @pl.when(me == 0)
        def _():
            target[:, pl.ds(0, width)] = zeros

        @pl.when(me == n - 1)
        def _():
            target[:, pl.ds(width + own, width)] = zeros

    def wait():
        @pl.when(me > 0)
        def _():
            low.wait_send()
            high.wait_recv()

        @pl.when(me < n - 1)
        def _():
            high.wait_send()
            low.wait_recv()

    return start, wait


def greet(me, n, everyone):
    barrier = pltpu.get_barrier_semaphore()
    if everyone:
        def one(step, carry):
            pl.semaphore_signal(
                barrier, inc=1, device_id={"row": lax.rem(me + step, n)},
                device_id_type=pl.DeviceIdType.MESH,
            )
            return carry

        lax.fori_loop(1, n, one, 0)
        pl.semaphore_wait(barrier, n - 1)
    else:
        for cond, who in neighbours(me, n):
            @pl.when(cond)
            def _():
                pl.semaphore_signal(
                    barrier, inc=1, device_id={"row": who}, device_id_type=pl.DeviceIdType.MESH
                )
        pl.semaphore_wait(barrier, jnp.minimum(me, 1) + jnp.minimum(n - 1 - me, 1))


def first_kernel(n, start_ref, vals_ref, cols_ref, cvals_ref,
                 ext_ref, lists_ref, dinv_ref, cdinv_ref, bounds_ref,
                 words, mine, theirs, sends, recvs, bsends, brecvs, own_sem):
    me = lax.axis_index("row")
    own = start_ref.shape[1]
    width = (ext_ref.shape[1] - own) // 2
    blocks, cblocks = own // LANE, cvals_ref.shape[3] // LANE
    greet(me, n, True)
    start, wait = exchange(start_ref, ext_ref, width, own, me, n, sends, recvs)
    start()
    keep = pltpu.make_async_copy(start_ref, ext_ref.at[:, pl.ds(width, own)], own_sem)
    keep.start()

    low = jnp.full((1, LANE), -jnp.inf, f32)

    def bound_step(g, best):
        for u in range(2):
            best = bound_of_block(vals_ref, at_block(g * 2 + u), dinv_ref, best)
        return best

    best = lax.fori_loop(0, blocks // 2, bound_step, low)
    cbest = low
    for b in range(cblocks):
        cbest = bound_of_block(cvals_ref, at_block(b), cdinv_ref, cbest)
    both = jnp.concatenate([jnp.broadcast_to(x, (4, LANE)) for x in (best, cbest)], axis=0)
    for shift in (64, 32, 16, 8, 4, 2, 1):
        both = jnp.maximum(both, pltpu.roll(both, shift, 1))
    mine[...] = both
    theirs[0] = both

    def copy_to(step):
        return pltpu.make_async_remote_copy(
            src_ref=mine,
            dst_ref=theirs.at[step],
            send_sem=bsends.at[step],
            recv_sem=brecvs.at[step],
            device_id={"row": lax.rem(me + step, n)},
            device_id_type=pl.DeviceIdType.MESH,
        )

    for step in range(1, n):
        copy_to(step).start()

    def word_step(b, carry):
        rows = pad_rows(cols_ref[:, at_block(b)] >> 7)
        bits = [jnp.left_shift(1, row & 31) for row in rows]
        for q in range(4):
            word = jnp.where((rows[0] >> 5) == q, bits[0], 0) | jnp.where((rows[1] >> 5) == q, bits[1], 0)
            word = word[0:4] | word[4:8]
            word = word[0:2] | word[2:4]
            words[q, pl.ds(b, 1), :] = word[0:1] | word[1:2]
        return carry

    lax.fori_loop(0, blocks, word_step, 0, unroll=4)
    lane = lax.broadcasted_iota(i32, (blocks, LANE), 1)
    chosen = jnp.zeros((blocks, LANE), i32)
    for q in range(4):
        word = words[q]
        for shift in (64, 32, 16, 8, 4, 2, 1):
            word = word | pltpu.roll(word, shift, 1)
        chosen = jnp.where((lane >> 5) == q, word, chosen)
    present = (jnp.right_shift(chosen, lane & 31) & 1).astype(f32).astype(bf16)
    tri = (
        lax.broadcasted_iota(i32, (LANE, LANE), 0) <= lax.broadcasted_iota(i32, (LANE, LANE), 1)
    ).astype(f32).astype(bf16)
    upto = jnp.dot(present, tri, preferred_element_type=f32).astype(i32)
    for s in range(blocks // 8):
        count = upto[8 * s : 8 * s + 8]
        slot = lane[0:8]
        found = jnp.zeros((8, LANE), i32)
        for step in (64, 32, 16, 8, 4, 2, 1):
            there = take_lanes(count, found + (step - 1))
            found = jnp.where(there <= slot, found + step, found)
        total = take_lanes(count, jnp.full((8, LANE), LANE - 1, i32))
        lists_ref[8 * s : 8 * s + 8, :] = found + total * 256

    for step in range(1, n):
        copy_to(step).wait()
    bounds_ref[...] = jnp.max(theirs[...], axis=0)
    keep.wait()
    wait()


def apply_into(out_ref, lists_ref, table_ref, vals_ref, cols_ref):
    blocks = cols_ref.shape[1] // LANE

    def group_step(g, carry):
        base = g * GROUP
        index = [halves(cols_ref[:, at_block(base + u)]) for u in range(GROUP)]
        most = lists_ref[base, 0]
        for u in range(1, GROUP):
            most = jnp.maximum(most, lists_ref[base + u, 0])
        chunks = ((most >> 8) + (CHUNK - 1)) // CHUNK

        def chunk_step(k, flat):
            flat = list(flat)
            for u in range(GROUP):
                acc = flat[6 * u : 6 * u + 6]
                for t in range(CHUNK):
                    r = lists_ref[base + u, k * CHUNK + t] & 255
                    acc = visit(table_ref, r, *index[u], acc)
                flat[6 * u : 6 * u + 6] = acc
            return tuple(flat)

        zero = jnp.zeros((8, LANE), f32)
        flat = chunk_step(0, (zero,) * (6 * GROUP))
        flat = lax.fori_loop(1, chunks, chunk_step, flat)
        for u in range(GROUP):
            at = at_block(base + u)
            for c, row in enumerate(contract(vals_ref, at, flat[6 * u : 6 * u + 6])):
                out_ref[c : c + 1, at] = row
        return carry

    lax.fori_loop(0, blocks // GROUP, group_step, 0)


def apply_start(lists_ref, ext_ref, vals_ref, cols_ref, rhs_ref, dinv_ref, bounds_ref,
                res_ref, first_ref, scratch):
    apply_into(scratch, lists_ref, ext_ref, vals_ref, cols_ref)
    theta = coefficients(bounds_ref[0:1, 0:1])[0]
    res = rhs_ref[...] - scratch[...]
    res_ref[...] = res
    first_ref[...] = dinv_ref[...] * res / theta


def apply_first(lists_ref, ext_ref, vals_ref, cols_ref, res_ref, dinv_ref, bounds_ref, first_ref,
                start_ref, res_out, second_ref, iterate_ref, scratch):
    apply_into(scratch, lists_ref, ext_ref, vals_ref, cols_ref)
    theta, delta, rho_zero, rho_one = coefficients(bounds_ref[0:1, 0:1])
    res = res_ref[...] - scratch[...]
    res_out[...] = res
    first = first_ref[...]
    second = (rho_one * rho_zero) * first + (2.0 * rho_one / delta) * dinv_ref[...] * res
    second_ref[...] = second
    iterate_ref[...] = start_ref[...] + first + second


def apply_second(lists_ref, ext_ref, vals_ref, cols_ref, res_ref, prol_ref, place_ref,
                 sums_ref, scratch):
    apply_into(scratch, lists_ref, ext_ref, vals_ref, cols_ref)
    count = scratch.shape[1]
    tiles = sums_ref.shape[1] // LANE
    piece = 8 * LANE

    def step(p, acc):
        at = pl.ds(pl.multiple_of(p * piece, piece), piece)
        res = res_ref[:, at] - scratch[:, at]
        contrib = jnp.zeros((3, piece), f32)
        for c in range(3):
            contrib = contrib + prol_ref[c, :, at].astype(f32) * res[c : c + 1]
        head = contrib.astype(bf16).astype(f32)
        tail = contrib - head
        both = jnp.concatenate([head, tail, jnp.zeros((2, piece), f32)], axis=0)
        place = place_ref[:, at]
        high = jnp.broadcast_to(place >> 7, (8, piece))
        rows = jnp.concatenate([jnp.where(high == h, both, 0.0) for h in range(tiles)], axis=0)
        hot = jnp.where(
            jnp.broadcast_to(place & (LANE - 1), (LANE, piece))
            == lax.broadcasted_iota(i32, (LANE, piece), 0),
            1.0,
            0.0,
        ).astype(bf16)
        return acc + lax.dot_general(
            rows.astype(bf16), hot, (((1,), (1,)), ((), ())), preferred_element_type=f32
        )

    acc = lax.fori_loop(0, count // piece, step, jnp.zeros((8 * tiles, LANE), f32))
    for h in range(tiles):
        part = acc[8 * h : 8 * h + 8]
        sums_ref[:, h * LANE : (h + 1) * LANE] = part[0:3] + part[3:6]


def coarse_kernel(n, sums_ref, vals_ref, cols_ref, dinv_ref, bounds_ref,
                  iterate_ref, res_ref, ghosts, d1, d2, t1, t2, sends, recvs):
    me = lax.axis_index("row")
    own = dinv_ref.shape[1]
    blocks = own // LANE
    width = own // 2
    greet(me, n, False)
    wide = own + 2 * LANE
    low = pltpu.make_async_remote_copy(
        src_ref=sums_ref.at[:, pl.ds(0, LANE)], dst_ref=ghosts.at[1],
        send_sem=sends.at[0], recv_sem=recvs.at[0],
        device_id={"row": jnp.maximum(me - 1, 0)}, device_id_type=pl.DeviceIdType.MESH,
    )
    high = pltpu.make_async_remote_copy(
        src_ref=sums_ref.at[:, pl.ds(wide - LANE, LANE)], dst_ref=ghosts.at[0],
        send_sem=sends.at[1], recv_sem=recvs.at[1],
        device_id={"row": jnp.minimum(me + 1, n - 1)}, device_id_type=pl.DeviceIdType.MESH,
    )
    zeros = jnp.zeros((3, LANE), f32)

    @pl.when(me > 0)
    def _():
        low.start()

    @pl.when(me < n - 1)
    def _():
        high.start()

    @pl.when(me == 0)
    def _():
        ghosts[0] = zeros

    @pl.when(me == n - 1)
    def _():
        ghosts[1] = zeros

    index = [halves(cols_ref[:, at_block(b)]) for b in range(blocks)]
    theta, delta, rho_zero, rho_one = coefficients(bounds_ref[4:5, 0:1])
    dinv = dinv_ref[...]

    @pl.when(me > 0)
    def _():
        low.wait_send()
        high.wait_recv()

    @pl.when(me < n - 1)
    def _():
        high.wait_send()
        low.wait_recv()

    tiles = [sums_ref[:, (h + 1) * LANE : (h + 2) * LANE] for h in range(blocks)]
    tiles[0] = tiles[0] + ghosts[0]
    tiles[-1] = tiles[-1] + ghosts[1]
    res = jnp.concatenate(tiles, axis=1)

    def apply(table):
        for b in range(blocks):
            acc = [jnp.zeros((8, LANE), f32)] * 6
            for r in range(2 * blocks):
                acc = visit(table, r, *index[b], acc)
            for c, row in enumerate(contract(vals_ref, at_block(b), acc)):
                res_ref[c : c + 1, at_block(b)] = row

    def swap(value, held, table, k):
        held[...] = value
        start, wait = exchange(
            held, table, width, own, me, n, sends.at[pl.ds(2 * k, 2)], recvs.at[pl.ds(2 * k, 2)]
        )
        start()
        table[:, pl.ds(width, own)] = value
        wait()

    first = dinv * res / theta
    swap(first, d1, t1, 1)
    apply(t1)
    res = res - res_ref[...]
    second = (rho_one * rho_zero) * first + (2.0 * rho_one / delta) * dinv * res
    swap(second, d2, t2, 2)
    iterate_ref[...] = first + second
    apply(t2)
    res_ref[...] = res - res_ref[...]


def params(collective=None):
    if collective is None:
        return pltpu.CompilerParams(vmem_limit_bytes=48 * 1024 * 1024)
    return pltpu.CompilerParams(
        vmem_limit_bytes=48 * 1024 * 1024, collective_id=collective, has_side_effects=True
    )


def halo_kernel(n, vector_ref, ext_ref, sends, recvs, own_sem):
    me = lax.axis_index("row")
    own = vector_ref.shape[1]
    width = (ext_ref.shape[1] - own) // 2
    greet(me, n, False)
    start, wait = exchange(vector_ref, ext_ref, width, own, me, n, sends, recvs)
    start()
    keep = pltpu.make_async_copy(vector_ref, ext_ref.at[:, pl.ds(width, own)], own_sem)
    keep.start()
    keep.wait()
    wait()


def shards(n, start, rhs, fine_vals, fine_cols, prol, aggregate, coarse_vals, coarse_cols):
    nf, nc = start.shape[1], coarse_vals.shape[3]
    blocks = nf // LANE
    shape = jax.ShapeDtypeStruct
    fine, ext = shape((3, nf), f32), shape((3, 2 * nf), f32)
    coarse = shape((3, nc), f32)
    dma = pltpu.SemaphoreType.DMA

    ext0, lists, dinv, cdinv, bounds = pl.pallas_call(
        functools.partial(first_kernel, n),
        out_shape=(ext, shape((blocks, LANE), i32), fine, coarse, shape((8, LANE), f32)),
        in_specs=[VMEM] * 4,
        out_specs=(VMEM,) * 5,
        scratch_shapes=[
            pltpu.VMEM((4, blocks, LANE), i32),
            pltpu.VMEM((8, LANE), f32),
            pltpu.VMEM((n, 8, LANE), f32),
            dma((2,)), dma((2,)), dma((n,)), dma((n,)), dma,
        ],
        compiler_params=params(0),
        name="prepare",
    )(start, fine_vals, fine_cols, coarse_vals)

    def halo(vector, collective):
        return pl.pallas_call(
            functools.partial(halo_kernel, n),
            out_shape=ext,
            in_specs=[VMEM],
            out_specs=VMEM,
            scratch_shapes=[dma((2,)), dma((2,)), dma],
            compiler_params=params(collective),
            name=f"halo{collective}",
        )(vector)

    def applied(kernel, outs, *args):
        return pl.pallas_call(
            kernel,
            out_shape=outs,
            in_specs=[SMEM] + [VMEM] * len(args),
            out_specs=(VMEM,) * len(outs),
            scratch_shapes=[pltpu.VMEM((3, nf), f32)],
            compiler_params=params(),
            name=kernel.__name__,
        )(lists, *args)

    res, first = applied(
        apply_start, (fine, fine), ext0, fine_vals, fine_cols, rhs, dinv, bounds
    )
    res, second, iterate = applied(
        apply_first, (fine, fine, fine), halo(first, 1), fine_vals, fine_cols, res, dinv, bounds,
        first, start,
    )
    place = (aggregate - (lax.axis_index("row") * nc - LANE)).reshape(1, nf)
    (sums,) = applied(
        apply_second, (shape((3, nc + 2 * LANE), f32),), halo(second, 2), fine_vals, fine_cols, res,
        prol, place,
    )
    coarse_iterate, coarse_residual = pl.pallas_call(
        functools.partial(coarse_kernel, n),
        out_shape=(coarse, coarse),
        in_specs=[VMEM] * 5,
        out_specs=(VMEM,) * 2,
        scratch_shapes=[
            pltpu.VMEM((2, 3, LANE), f32),
            pltpu.VMEM((3, nc), f32), pltpu.VMEM((3, nc), f32),
            pltpu.VMEM((3, 2 * nc), f32), pltpu.VMEM((3, 2 * nc), f32),
            dma((6,)), dma((6,)),
        ],
        compiler_params=params(3),
        name="coarse",
    )(sums, coarse_vals, coarse_cols, cdinv, bounds)
    return (iterate, coarse_iterate, coarse_residual)


def solution(mesh):
    in_specs = (
        P(None, ("grp", "row")),
        P(None, ("grp", "row")),
        P(None, None, None, ("grp", "row")),
        P(None, ("grp", "row")),
        P(None, None, ("grp", "row")),
        P(("grp", "row")),
        P(None, None, None, ("grp", "row")),
        P(None, ("grp", "row")),
    )
    out_specs = (P(None, ("grp", "row")), P(None, ("grp", "row")), P(None, ("grp", "row")))
    return jax.shard_map(
        functools.partial(shards, mesh.shape["row"]),
        mesh=mesh, in_specs=in_specs, out_specs=out_specs, check_vma=False,
    )
```

```python
import functools

import jax
import jax.numpy as jnp
from jax import lax
from jax.experimental import pallas as pl
from jax.experimental.pallas import tpu as pltpu
from jax.sharding import PartitionSpec as P

LANE = 128
CHUNK = 16
PAIRS = 2
STEPS = float(2**20 - 1)
lower_fraction = 0.1

f32, i32, bf16 = jnp.float32, jnp.int32, jnp.bfloat16
VMEM = pl.BlockSpec(memory_space=pltpu.VMEM)
SMEM = pl.BlockSpec(memory_space=pltpu.SMEM)
HBM = pl.BlockSpec(memory_space=pltpu.HBM)


def coefficients(bound):
    lowest = lower_fraction * bound
    theta = (bound + lowest) / 2.0
    delta = (bound - lowest) / 2.0
    sigma = theta / delta
    rho_zero = 1.0 / sigma
    rho_one = 1.0 / (2.0 * sigma - rho_zero)
    return (theta, delta, rho_zero, rho_one)


def at_block(b):
    if isinstance(b, int):
        return pl.ds(b * LANE, LANE)
    return pl.ds(pl.multiple_of(b * LANE, LANE), LANE)


def take_lanes(row, lanes):
    return jnp.take_along_axis(row, lanes, axis=1, mode="promise_in_bounds")


def pad_rows(x):
    return x[0:8], jnp.concatenate([x[8:12], x[8:12]], axis=0)


def halves(cols):
    parts = pad_rows(cols)
    return [p & (LANE - 1) for p in parts], [p >> 7 for p in parts]


def pair_index(cols_ref, p):
    cols = [cols_ref[:, at_block(2 * p + u)] for u in range(2)]
    rel = [((c >> 7) - (2 * p + u)) & (LANE - 1) for u, c in enumerate(cols)]
    lanes = [c & (LANE - 1) for c in cols]
    return [
        (x[0][0:8], x[1][0:8], jnp.concatenate([x[0][8:12], x[1][8:12]], axis=0))
        for x in (lanes, rel)
    ]


def visit_pair(table_ref, p, r, lanes, rows, upper, acc):
    masks = [row == r for row in rows]
    out = []
    for w in range(2):
        first, second = [
            jnp.broadcast_to(table_ref[w : w + 1, at_block((2 * p + u + r) & (LANE - 1))], (8, LANE))
            for u in range(2)
        ]
        for h, src in enumerate((first, second, jnp.where(upper, first, second))):
            out.append(jnp.where(masks[h], take_lanes(src, lanes[h]), acc[3 * w + h]))
    return out


def pack(ext_ref, table_ref):
    vector = ext_ref[...]
    most = jnp.max(jnp.max(jnp.abs(vector), axis=1, keepdims=True), axis=0, keepdims=True)
    most = jnp.maximum(most, 1e-30)
    fixed = jnp.round(vector * (STEPS / most)).astype(i32)
    third = fixed[2:3] + 2**20
    table_ref[...] = jnp.left_shift(fixed[0:2], 11) | jnp.concatenate(
        [third >> 10, third & 1023], axis=0
    )
    return most / STEPS


def unpack(words):
    one, two = words
    third = (jnp.left_shift(one & 2047, 10) | (two & 1023)) - 2**20
    return [x.astype(f32) for x in (one >> 11, two >> 11, third)]


def visit(table_ref, r, lanes, rows, acc):
    at = at_block(r)
    masks = [row == r for row in rows]
    out = []
    for j in range(3):
        src = jnp.broadcast_to(table_ref[j : j + 1, at], (8, LANE))
        for h in range(2):
            out.append(jnp.where(masks[h], take_lanes(src, lanes[h]), acc[2 * j + h]))
    return out


def contract(vals_ref, at, gathered):
    out = []
    for c in range(3):
        total = None
        for j in range(3):
            term = vals_ref[c, j, :, at].astype(f32) * gathered[j]
            total = term if total is None else total + term
        out.append(jnp.sum(total, axis=0, keepdims=True))
    return out


def bound_of_block(vals_ref, at, dinv_ref, best):
    for c in range(3):
        total = None
        for j in range(3):
            term = jnp.abs(vals_ref[c, j, :, at].astype(f32))
            total = term if total is None else total + term
        inverse = 1.0 / vals_ref[c, c, :, at].astype(f32)[0:1]
        dinv_ref[c : c + 1, at] = inverse
        best = jnp.maximum(best, jnp.sum(total, axis=0, keepdims=True) * inverse)
    return best


def neighbours(me, n):
    return ((me > 0, me - 1), (me < n - 1, me + 1))


def exchange(source, target, width, own, me, n, sends, recvs):
    low = pltpu.make_async_remote_copy(
        src_ref=source.at[:, pl.ds(0, width)],
        dst_ref=target.at[:, pl.ds(width + own, width)],
        send_sem=sends.at[0],
        recv_sem=recvs.at[0],
        device_id={"row": jnp.maximum(me - 1, 0)},
        device_id_type=pl.DeviceIdType.MESH,
    )
    high = pltpu.make_async_remote_copy(
        src_ref=source.at[:, pl.ds(own - width, width)],
        dst_ref=target.at[:, pl.ds(0, width)],
        send_sem=sends.at[1],
        recv_sem=recvs.at[1],
        device_id={"row": jnp.minimum(me + 1, n - 1)},
        device_id_type=pl.DeviceIdType.MESH,
    )

    def start():
        @pl.when(me > 0)
        def _():
            low.start()

        @pl.when(me < n - 1)
        def _():
            high.start()

        zeros = jnp.zeros((3, width), f32)

        @pl.when(me == 0)
        def _():
            target[:, pl.ds(0, width)] = zeros

        @pl.when(me == n - 1)
        def _():
            target[:, pl.ds(width + own, width)] = zeros

    def wait():
        @pl.when(me > 0)
        def _():
            low.wait_send()
            high.wait_recv()

        @pl.when(me < n - 1)
        def _():
            high.wait_send()
            low.wait_recv()

    return start, wait


def greet(me, n, everyone, between=lambda: None):
    barrier = pltpu.get_barrier_semaphore()
    if everyone:
        def one(step, carry):
            pl.semaphore_signal(
                barrier, inc=1, device_id={"row": lax.rem(me + step, n)},
                device_id_type=pl.DeviceIdType.MESH,
            )
            return carry

        lax.fori_loop(1, n, one, 0)
        between()
        pl.semaphore_wait(barrier, n - 1)
    else:
        for cond, who in neighbours(me, n):
            @pl.when(cond)
            def _():
                pl.semaphore_signal(
                    barrier, inc=1, device_id={"row": who}, device_id_type=pl.DeviceIdType.MESH
                )
        between()
        pl.semaphore_wait(barrier, jnp.minimum(me, 1) + jnp.minimum(n - 1 - me, 1))


def first_kernel(n, start_hbm, vals_hbm, cols_hbm, cvals_hbm,
                 ext_ref, lists_ref, dinv_ref, cdinv_ref, bounds_ref,
                 vals_ref, cols_ref, cvals_ref, words, mine, theirs,
                 sends, recvs, bsends, brecvs, local):
    me = lax.axis_index("row")
    own = start_hbm.shape[1]
    width = (ext_ref.shape[1] - own) // 2
    blocks, cblocks = own // LANE, cvals_ref.shape[3] // LANE
    part = own // 4
    fetch_vals = [
        pltpu.make_async_copy(
            vals_hbm.at[:, :, :, pl.ds(p * part, part)],
            vals_ref.at[:, :, :, pl.ds(p * part, part)],
            local.at[p],
        )
        for p in range(4)
    ]
    fetch_cvals = pltpu.make_async_copy(cvals_hbm, cvals_ref, local.at[4])
    fetch_cols = pltpu.make_async_copy(cols_hbm, cols_ref, local.at[5])
    keep = pltpu.make_async_copy(start_hbm, ext_ref.at[:, pl.ds(width, own)], local.at[6])
    for copy in (*fetch_vals, fetch_cvals, fetch_cols, keep):
        copy.start()
    start, wait = exchange(start_hbm, ext_ref, width, own, me, n, sends, recvs)

    def bounds():
        low = jnp.full((1, LANE), -jnp.inf, f32)

        def bound_step(g, best):
            for u in range(4):
                best = bound_of_block(vals_ref, at_block(g * 4 + u), dinv_ref, best)
            return best

        best = low
        for p in range(4):
            fetch_vals[p].wait()
            best = lax.fori_loop(p * (blocks // 16), (p + 1) * (blocks // 16), bound_step, best)
        fetch_cvals.wait()
        cbest = low
        for b in range(cblocks):
            cbest = bound_of_block(cvals_ref, at_block(b), cdinv_ref, cbest)
        both = jnp.concatenate([jnp.broadcast_to(x, (4, LANE)) for x in (best, cbest)], axis=0)
        for shift in (64, 32, 16, 8, 4, 2, 1):
            both = jnp.maximum(both, pltpu.roll(both, shift, 1))
        mine[...] = both
        theirs[0] = both

    greet(me, n, True, bounds)
    start()

    def copy_to(step):
        return pltpu.make_async_remote_copy(
            src_ref=mine,
            dst_ref=theirs.at[step],
            send_sem=bsends.at[step],
            recv_sem=brecvs.at[step],
            device_id={"row": lax.rem(me + step, n)},
            device_id_type=pl.DeviceIdType.MESH,
        )

    for step in range(1, n):
        copy_to(step).start()

    fetch_cols.wait()
    pairs = blocks // 2

    def word_step(p, carry):
        _, rows = pair_index(cols_ref, p)
        bits = [jnp.left_shift(1, row & 31) for row in rows]
        for q in range(4):
            word = functools.reduce(
                jnp.bitwise_or, [jnp.where((rows[h] >> 5) == q, bits[h], 0) for h in range(3)]
            )
            word = word[0:4] | word[4:8]
            word = word[0:2] | word[2:4]
            words[q, pl.ds(p, 1), :] = word[0:1] | word[1:2]
        return carry

    lax.fori_loop(0, pairs, word_step, 0, unroll=4)
    lane = lax.broadcasted_iota(i32, (pairs, LANE), 1)
    chosen = jnp.zeros((pairs, LANE), i32)
    for q in range(4):
        word = words[q]
        for shift in (64, 32, 16, 8, 4, 2, 1):
            word = word | pltpu.roll(word, shift, 1)
        chosen = jnp.where((lane >> 5) == q, word, chosen)
    present = (jnp.right_shift(chosen, lane & 31) & 1).astype(f32).astype(bf16)
    tri = (
        lax.broadcasted_iota(i32, (LANE, LANE), 0) <= lax.broadcasted_iota(i32, (LANE, LANE), 1)
    ).astype(f32).astype(bf16)
    upto = jnp.dot(present, tri, preferred_element_type=f32).astype(i32)
    for s in range(pairs // 8):
        count = upto[8 * s : 8 * s + 8]
        slot = lane[0:8]
        found = jnp.zeros((8, LANE), i32)
        for step in (64, 32, 16, 8, 4, 2, 1):
            there = take_lanes(count, found + (step - 1))
            found = jnp.where(there <= slot, found + step, found)
        total = take_lanes(count, jnp.full((8, LANE), LANE - 1, i32))
        lists_ref[8 * s : 8 * s + 8, :] = found + total * 256

    for step in range(1, n):
        copy_to(step).wait()
    bounds_ref[...] = jnp.max(theirs[...], axis=0)
    keep.wait()
    wait()


def apply_into(out_ref, table_ref, lists_ref, ext_ref, vals_ref, cols_ref):
    unit = pack(ext_ref, table_ref)
    upper = lax.broadcasted_iota(i32, (8, LANE), 0) < 4

    def group_step(g, carry):
        base = g * PAIRS
        index = [pair_index(cols_ref, base + u) for u in range(PAIRS)]
        most = lists_ref[base, 0]
        for u in range(1, PAIRS):
            most = jnp.maximum(most, lists_ref[base + u, 0])
        chunks = ((most >> 8) + (CHUNK - 1)) // CHUNK

        def chunk_step(k, flat):
            flat = list(flat)
            for u in range(PAIRS):
                acc = flat[6 * u : 6 * u + 6]
                for t in range(CHUNK):
                    r = lists_ref[base + u, k * CHUNK + t] & 255
                    acc = visit_pair(table_ref, base + u, r, *index[u], upper, acc)
                flat[6 * u : 6 * u + 6] = acc
            return tuple(flat)

        zero = jnp.zeros((8, LANE), i32)
        flat = chunk_step(0, (zero,) * (6 * PAIRS))
        flat = lax.fori_loop(1, chunks, chunk_step, flat)
        for u in range(PAIRS):
            parts = [unpack((flat[6 * u + h], flat[6 * u + 3 + h])) for h in range(3)]
            for v in range(2):
                at = at_block(2 * (base + u) + v)
                gathered = [
                    jnp.concatenate([parts[v][j], parts[2][j][4 * v : 4 * v + 4]], axis=0)
                    for j in range(3)
                ]
                for c, row in enumerate(contract(vals_ref, at, gathered)):
                    out_ref[c : c + 1, at] = row
        return carry

    lax.fori_loop(0, cols_ref.shape[1] // (2 * LANE * PAIRS), group_step, 0)
    return unit


def apply_start(lists_ref, ext_ref, vals_ref, cols_ref, rhs_ref, dinv_ref, bounds_ref,
                res_ref, first_ref, scratch, table):
    unit = apply_into(scratch, table, lists_ref, ext_ref, vals_ref, cols_ref)
    theta = coefficients(bounds_ref[0:1, 0:1])[0]
    res = rhs_ref[...] - unit * scratch[...]
    res_ref[...] = res
    first_ref[...] = dinv_ref[...] * res / theta


def apply_first(lists_ref, ext_ref, vals_ref, cols_ref, res_ref, dinv_ref, bounds_ref, first_ref,
                start_ref, res_out, second_ref, iterate_ref, scratch, table):
    unit = apply_into(scratch, table, lists_ref, ext_ref, vals_ref, cols_ref)
    theta, delta, rho_zero, rho_one = coefficients(bounds_ref[0:1, 0:1])
    res = res_ref[...] - unit * scratch[...]
    res_out[...] = res
    first = first_ref[...]
    second = (rho_one * rho_zero) * first + (2.0 * rho_one / delta) * dinv_ref[...] * res
    second_ref[...] = second
    iterate_ref[...] = start_ref[...] + first + second


def apply_second(lists_ref, ext_ref, vals_ref, cols_ref, res_ref, prol_ref, place_ref,
                 sums_ref, scratch, table):
    unit = apply_into(scratch, table, lists_ref, ext_ref, vals_ref, cols_ref)
    count = scratch.shape[1]
    tiles = sums_ref.shape[1] // LANE
    piece = 8 * LANE
    offset = lax.axis_index("row") * (sums_ref.shape[1] - 2 * LANE) - LANE

    def step(p, acc):
        at = pl.ds(pl.multiple_of(p * piece, piece), piece)
        res = res_ref[:, at] - unit * scratch[:, at]
        contrib = jnp.zeros((3, piece), f32)
        for c in range(3):
            contrib = contrib + prol_ref[c, :, at].astype(f32) * res[c : c + 1]
        head = contrib.astype(bf16).astype(f32)
        tail = contrib - head
        both = jnp.concatenate([head, tail, jnp.zeros((2, piece), f32)], axis=0)
        place = place_ref[:, at] - offset
        high = jnp.broadcast_to(place >> 7, (8, piece))
        rows = jnp.concatenate([jnp.where(high == h, both, 0.0) for h in range(tiles)], axis=0)
        hot = jnp.where(
            jnp.broadcast_to(place & (LANE - 1), (LANE, piece))
            == lax.broadcasted_iota(i32, (LANE, piece), 0),
            1.0,
            0.0,
        ).astype(bf16)
        return acc + lax.dot_general(
            rows.astype(bf16), hot, (((1,), (1,)), ((), ())), preferred_element_type=f32
        )

    acc = lax.fori_loop(0, count // piece, step, jnp.zeros((8 * tiles, LANE), f32))
    for h in range(tiles):
        part = acc[8 * h : 8 * h + 8]
        sums_ref[:, h * LANE : (h + 1) * LANE] = part[0:3] + part[3:6]


def coarse_kernel(n, sums_ref, vals_ref, cols_ref, dinv_ref, bounds_ref,
                  iterate_ref, res_ref, ghosts, d1, d2, t1, t2, sends, recvs):
    me = lax.axis_index("row")
    own = dinv_ref.shape[1]
    blocks = own // LANE
    width = own // 2
    greet(me, n, False)
    wide = own + 2 * LANE
    low = pltpu.make_async_remote_copy(
        src_ref=sums_ref.at[:, pl.ds(0, LANE)], dst_ref=ghosts.at[1],
        send_sem=sends.at[0], recv_sem=recvs.at[0],
        device_id={"row": jnp.maximum(me - 1, 0)}, device_id_type=pl.DeviceIdType.MESH,
    )
    high = pltpu.make_async_remote_copy(
        src_ref=sums_ref.at[:, pl.ds(wide - LANE, LANE)], dst_ref=ghosts.at[0],
        send_sem=sends.at[1], recv_sem=recvs.at[1],
        device_id={"row": jnp.minimum(me + 1, n - 1)}, device_id_type=pl.DeviceIdType.MESH,
    )
    zeros = jnp.zeros((3, LANE), f32)

    @pl.when(me > 0)
    def _():
        low.start()

    @pl.when(me < n - 1)
    def _():
        high.start()

    @pl.when(me == 0)
    def _():
        ghosts[0] = zeros

    @pl.when(me == n - 1)
    def _():
        ghosts[1] = zeros

    index = [halves(cols_ref[:, at_block(b)]) for b in range(blocks)]
    theta, delta, rho_zero, rho_one = coefficients(bounds_ref[4:5, 0:1])
    dinv = dinv_ref[...]

    @pl.when(me > 0)
    def _():
        low.wait_send()
        high.wait_recv()

    @pl.when(me < n - 1)
    def _():
        high.wait_send()
        low.wait_recv()

    tiles = [sums_ref[:, (h + 1) * LANE : (h + 2) * LANE] for h in range(blocks)]
    tiles[0] = tiles[0] + ghosts[0]
    tiles[-1] = tiles[-1] + ghosts[1]
    res = jnp.concatenate(tiles, axis=1)

    def apply(table):
        for b in range(blocks):
            acc = [jnp.zeros((8, LANE), f32)] * 6
            for r in range(2 * blocks):
                acc = visit(table, r, *index[b], acc)
            gathered = [jnp.concatenate([acc[2 * j], acc[2 * j + 1][0:4]], axis=0) for j in range(3)]
            for c, row in enumerate(contract(vals_ref, at_block(b), gathered)):
                res_ref[c : c + 1, at_block(b)] = row

    def swap(value, held, table, k):
        held[...] = value
        start, wait = exchange(
            held, table, width, own, me, n, sends.at[pl.ds(2 * k, 2)], recvs.at[pl.ds(2 * k, 2)]
        )
        start()
        table[:, pl.ds(width, own)] = value
        wait()

    first = dinv * res / theta
    swap(first, d1, t1, 1)
    apply(t1)
    res = res - res_ref[...]
    second = (rho_one * rho_zero) * first + (2.0 * rho_one / delta) * dinv * res
    swap(second, d2, t2, 2)
    iterate_ref[...] = first + second
    apply(t2)
    res_ref[...] = res - res_ref[...]


def params(collective=None):
    if collective is None:
        return pltpu.CompilerParams(vmem_limit_bytes=24 * 1024 * 1024)
    return pltpu.CompilerParams(
        vmem_limit_bytes=24 * 1024 * 1024, collective_id=collective, has_side_effects=True
    )


def halo_kernel(n, vector_ref, ext_ref, sends, recvs, own_sem):
    me = lax.axis_index("row")
    own = vector_ref.shape[1]
    width = (ext_ref.shape[1] - own) // 2
    greet(me, n, False)
    start, wait = exchange(vector_ref, ext_ref, width, own, me, n, sends, recvs)
    start()
    keep = pltpu.make_async_copy(vector_ref, ext_ref.at[:, pl.ds(width, own)], own_sem)
    keep.start()
    keep.wait()
    wait()


def shards(n, start, rhs, fine_vals, fine_cols, prol, aggregate, coarse_vals, coarse_cols):
    nf, nc = start.shape[1], coarse_vals.shape[3]
    blocks = nf // LANE
    shape = jax.ShapeDtypeStruct
    fine, ext = shape((3, nf), f32), shape((3, 2 * nf), f32)
    coarse = shape((3, nc), f32)
    dma = pltpu.SemaphoreType.DMA

    ext0, lists, dinv, cdinv, bounds = pl.pallas_call(
        functools.partial(first_kernel, n),
        out_shape=(ext, shape((blocks // 2, LANE), i32), fine, coarse, shape((8, LANE), f32)),
        in_specs=[HBM] * 4,
        out_specs=(VMEM,) * 5,
        scratch_shapes=[
            pltpu.VMEM(fine_vals.shape, bf16),
            pltpu.VMEM(fine_cols.shape, i32),
            pltpu.VMEM(coarse_vals.shape, bf16),
            pltpu.VMEM((4, blocks // 2, LANE), i32),
            pltpu.VMEM((8, LANE), f32),
            pltpu.VMEM((n, 8, LANE), f32),
            dma((2,)), dma((2,)), dma((n,)), dma((n,)), dma((7,)),
        ],
        compiler_params=params(0),
        name="prepare",
    )(start, fine_vals, fine_cols, coarse_vals)

    def halo(vector, collective):
        return pl.pallas_call(
            functools.partial(halo_kernel, n),
            out_shape=ext,
            in_specs=[VMEM],
            out_specs=VMEM,
            scratch_shapes=[dma((2,)), dma((2,)), dma],
            compiler_params=params(collective),
            name=f"halo{collective}",
        )(vector)

    def applied(kernel, outs, *args):
        return pl.pallas_call(
            kernel,
            out_shape=outs,
            in_specs=[SMEM] + [VMEM] * len(args),
            out_specs=(VMEM,) * len(outs),
            scratch_shapes=[pltpu.VMEM((3, nf), f32), pltpu.VMEM((2, 2 * nf), i32)],
            compiler_params=params(),
            name=kernel.__name__,
        )(lists, *args)

    res, first = applied(
        apply_start, (fine, fine), ext0, fine_vals, fine_cols, rhs, dinv, bounds
    )
    res, second, iterate = applied(
        apply_first, (fine, fine, fine), halo(first, 1), fine_vals, fine_cols, res, dinv, bounds,
        first, start,
    )
    place = aggregate.reshape(1, nf)
    (sums,) = applied(
        apply_second, (shape((3, nc + 2 * LANE), f32),), halo(second, 2), fine_vals, fine_cols, res,
        prol, place,
    )
    coarse_iterate, coarse_residual = pl.pallas_call(
        functools.partial(coarse_kernel, n),
        out_shape=(coarse, coarse),
        in_specs=[VMEM] * 5,
        out_specs=(VMEM,) * 2,
        scratch_shapes=[
            pltpu.VMEM((2, 3, LANE), f32),
            pltpu.VMEM((3, nc), f32), pltpu.VMEM((3, nc), f32),
            pltpu.VMEM((3, 2 * nc), f32), pltpu.VMEM((3, 2 * nc), f32),
            dma((6,)), dma((6,)),
        ],
        compiler_params=params(3),
        name="coarse",
    )(sums, coarse_vals, coarse_cols, cdinv, bounds)
    return (iterate, coarse_iterate, coarse_residual)


def solution(mesh):
    in_specs = (
        P(None, ("grp", "row")),
        P(None, ("grp", "row")),
        P(None, None, None, ("grp", "row")),
        P(None, ("grp", "row")),
        P(None, None, ("grp", "row")),
        P(("grp", "row")),
        P(None, None, None, ("grp", "row")),
        P(None, ("grp", "row")),
    )
    out_specs = (P(None, ("grp", "row")), P(None, ("grp", "row")), P(None, ("grp", "row")))
    return jax.shard_map(
        functools.partial(shards, mesh.shape["row"]),
        mesh=mesh, in_specs=in_specs, out_specs=out_specs, check_vma=False,
    )
```

```python
import functools

import jax
import jax.numpy as jnp
from jax import lax
from jax.experimental import pallas as pl
from jax.experimental.pallas import tpu as pltpu
from jax.sharding import PartitionSpec as P

LANE = 128
CHUNK = 16
PAIRS = 2
STEPS = float(2**20 - 1)
lower_fraction = 0.1

f32, i32, bf16 = jnp.float32, jnp.int32, jnp.bfloat16
VMEM = pl.BlockSpec(memory_space=pltpu.VMEM)
SMEM = pl.BlockSpec(memory_space=pltpu.SMEM)
HBM = pl.BlockSpec(memory_space=pltpu.HBM)


def coefficients(bound):
    lowest = lower_fraction * bound
    theta = (bound + lowest) / 2.0
    delta = (bound - lowest) / 2.0
    sigma = theta / delta
    rho_zero = 1.0 / sigma
    rho_one = 1.0 / (2.0 * sigma - rho_zero)
    return (theta, delta, rho_zero, rho_one)


def at_block(b):
    if isinstance(b, int):
        return pl.ds(b * LANE, LANE)
    return pl.ds(pl.multiple_of(b * LANE, LANE), LANE)


def take_lanes(row, lanes):
    return jnp.take_along_axis(row, lanes, axis=1, mode="promise_in_bounds")


def pad_rows(x):
    return x[0:8], jnp.concatenate([x[8:12], x[8:12]], axis=0)


def halves(cols):
    parts = pad_rows(cols)
    return [p & (LANE - 1) for p in parts], [p >> 7 for p in parts]


def pair_index(cols_ref, p):
    cols = [cols_ref[:, at_block(2 * p + u)] for u in range(2)]
    rel = [((c >> 7) - u) & (LANE - 1) for u, c in enumerate(cols)]
    lanes = [c & (LANE - 1) for c in cols]
    return [
        (x[0][0:8], x[1][0:8], jnp.concatenate([x[0][8:12], x[1][8:12]], axis=0))
        for x in (lanes, rel)
    ]


def visit_pair(table_ref, wanted, lanes, rows, upper, acc):
    acc = list(acc)
    for h in range(3):
        for r in wanted:
            mask = rows[h] == r
            for w in range(2):
                two = table_ref[w : w + 1, pl.ds(pl.multiple_of(r * LANE, LANE), 2 * LANE)]
                first = jnp.broadcast_to(two[:, :LANE], (8, LANE))
                second = jnp.broadcast_to(two[:, LANE:], (8, LANE))
                src = (first, second, None)[h]
                if src is None:
                    src = jnp.where(upper, first, second)
                acc[3 * w + h] = jnp.where(mask, take_lanes(src, lanes[h]), acc[3 * w + h])
    return acc


def pack(ext_ref, table_ref):
    size = ext_ref.shape[1]
    piece = 16 * LANE

    def at(p):
        return pl.ds(pl.multiple_of(p * piece, piece), piece)

    def largest(p, most):
        return jnp.maximum(most, jnp.abs(ext_ref[:, at(p)]))

    most = lax.fori_loop(0, size // piece, largest, jnp.zeros((3, piece), f32))
    most = jnp.max(jnp.max(most, axis=1, keepdims=True), axis=0, keepdims=True)
    most = jnp.maximum(most, 1e-30)
    scale = STEPS / most

    def words(vector):
        fixed = jnp.round(vector * scale).astype(i32)
        third = jnp.broadcast_to(fixed[2:3] + 2**20, (2, vector.shape[1]))
        head = lax.broadcasted_iota(i32, third.shape, 0) == 0
        return jnp.left_shift(fixed[0:2], 11) | jnp.where(head, third >> 10, third & 1023)

    def step(p, carry):
        table_ref[:, at(p)] = words(ext_ref[:, at(p)])
        return carry

    lax.fori_loop(0, size // piece, step, 0)
    table_ref[:, size : size + LANE] = table_ref[:, 0:LANE]
    return most / STEPS


def unpack(words):
    one, two = words
    third = (jnp.left_shift(one & 2047, 10) | (two & 1023)) - 2**20
    return [x.astype(f32) for x in (one >> 11, two >> 11, third)]


def visit(table_ref, r, lanes, rows, acc):
    at = at_block(r)
    masks = [row == r for row in rows]
    out = []
    for j in range(3):
        src = jnp.broadcast_to(table_ref[j : j + 1, at], (8, LANE))
        for h in range(2):
            out.append(jnp.where(masks[h], take_lanes(src, lanes[h]), acc[2 * j + h]))
    return out


def contract(vals_ref, at, gathered):
    out = []
    for c in range(3):
        total = None
        for j in range(3):
            term = vals_ref[c, j, :, at].astype(f32) * gathered[j]
            total = term if total is None else total + term
        out.append(jnp.sum(total, axis=0, keepdims=True))
    return out


def bound_of_block(vals_ref, at, dinv_ref, best):
    for c in range(3):
        total = None
        for j in range(3):
            term = jnp.abs(vals_ref[c, j, :, at].astype(f32))
            total = term if total is None else total + term
        inverse = 1.0 / vals_ref[c, c, :, at].astype(f32)[0:1]
        dinv_ref[c : c + 1, at] = inverse
        best = jnp.maximum(best, jnp.sum(total, axis=0, keepdims=True) * inverse)
    return best


def neighbours(me, n):
    return ((me > 0, me - 1), (me < n - 1, me + 1))


def exchange(source, target, width, own, me, n, sends, recvs):
    low = pltpu.make_async_remote_copy(
        src_ref=source.at[:, pl.ds(0, width)],
        dst_ref=target.at[:, pl.ds(width + own, width)],
        send_sem=sends.at[0],
        recv_sem=recvs.at[0],
        device_id={"row": jnp.maximum(me - 1, 0)},
        device_id_type=pl.DeviceIdType.MESH,
    )
    high = pltpu.make_async_remote_copy(
        src_ref=source.at[:, pl.ds(own - width, width)],
        dst_ref=target.at[:, pl.ds(0, width)],
        send_sem=sends.at[1],
        recv_sem=recvs.at[1],
        device_id={"row": jnp.minimum(me + 1, n - 1)},
        device_id_type=pl.DeviceIdType.MESH,
    )

    def start():
        @pl.when(me > 0)
        def _():
            low.start()

        @pl.when(me < n - 1)
        def _():
            high.start()

        zeros = jnp.zeros((3, width), f32)

        @pl.when(me == 0)
        def _():
            target[:, pl.ds(0, width)] = zeros

        @pl.when(me == n - 1)
        def _():
            target[:, pl.ds(width + own, width)] = zeros

    def wait():
        @pl.when(me > 0)
        def _():
            low.wait_send()
            high.wait_recv()

        @pl.when(me < n - 1)
        def _():
            high.wait_send()
            low.wait_recv()

    return start, wait


def greet(me, n, everyone, between=lambda: None):
    barrier = pltpu.get_barrier_semaphore()
    if everyone:
        def one(step, carry):
            pl.semaphore_signal(
                barrier, inc=1, device_id={"row": lax.rem(me + step, n)},
                device_id_type=pl.DeviceIdType.MESH,
            )
            return carry

        lax.fori_loop(1, n, one, 0)
        between()
        pl.semaphore_wait(barrier, n - 1)
    else:
        for cond, who in neighbours(me, n):
            @pl.when(cond)
            def _():
                pl.semaphore_signal(
                    barrier, inc=1, device_id={"row": who}, device_id_type=pl.DeviceIdType.MESH
                )
        between()
        pl.semaphore_wait(barrier, jnp.minimum(me, 1) + jnp.minimum(n - 1 - me, 1))


def first_kernel(n, start_hbm, vals_hbm, cols_hbm, cvals_hbm,
                 ext_ref, lists_ref, dinv_ref, cdinv_ref, bounds_ref,
                 vals_ref, cols_ref, cvals_ref, words, mine, theirs,
                 sends, recvs, bsends, brecvs, local):
    me = lax.axis_index("row")
    own = start_hbm.shape[1]
    width = (ext_ref.shape[1] - own) // 2
    blocks, cblocks = own // LANE, cvals_ref.shape[3] // LANE
    part = own // 4
    fetch_vals = [
        pltpu.make_async_copy(
            vals_hbm.at[:, :, :, pl.ds(p * part, part)],
            vals_ref.at[:, :, :, pl.ds(p * part, part)],
            local.at[p],
        )
        for p in range(4)
    ]
    fetch_cvals = pltpu.make_async_copy(cvals_hbm, cvals_ref, local.at[4])
    fetch_cols = pltpu.make_async_copy(cols_hbm, cols_ref, local.at[5])
    keep = pltpu.make_async_copy(start_hbm, ext_ref.at[:, pl.ds(width, own)], local.at[6])
    for copy in (*fetch_vals, fetch_cvals, fetch_cols, keep):
        copy.start()
    start, wait = exchange(start_hbm, ext_ref, width, own, me, n, sends, recvs)

    def bounds():
        low = jnp.full((1, LANE), -jnp.inf, f32)

        def bound_step(g, best):
            for u in range(4):
                best = bound_of_block(vals_ref, at_block(g * 4 + u), dinv_ref, best)
            return best

        best = low
        for p in range(4):
            fetch_vals[p].wait()
            best = lax.fori_loop(p * (blocks // 16), (p + 1) * (blocks // 16), bound_step, best)
        fetch_cvals.wait()
        cbest = low
        for b in range(cblocks):
            cbest = bound_of_block(cvals_ref, at_block(b), cdinv_ref, cbest)
        both = jnp.concatenate([jnp.broadcast_to(x, (4, LANE)) for x in (best, cbest)], axis=0)
        for shift in (64, 32, 16, 8, 4, 2, 1):
            both = jnp.maximum(both, pltpu.roll(both, shift, 1))
        mine[...] = both
        theirs[0] = both

    greet(me, n, True, bounds)
    start()

    def copy_to(step):
        return pltpu.make_async_remote_copy(
            src_ref=mine,
            dst_ref=theirs.at[step],
            send_sem=bsends.at[step],
            recv_sem=brecvs.at[step],
            device_id={"row": lax.rem(me + step, n)},
            device_id_type=pl.DeviceIdType.MESH,
        )

    for step in range(1, n):
        copy_to(step).start()

    fetch_cols.wait()
    pairs = blocks // 2

    def word_step(p, carry):
        _, rows = pair_index(cols_ref, p)
        bits = [jnp.left_shift(1, row & 31) for row in rows]
        for q in range(4):
            word = functools.reduce(
                jnp.bitwise_or, [jnp.where((rows[h] >> 5) == q, bits[h], 0) for h in range(3)]
            )
            word = word[0:4] | word[4:8]
            word = word[0:2] | word[2:4]
            words[q, pl.ds(p, 1), :] = word[0:1] | word[1:2]
        return carry

    lax.fori_loop(0, pairs, word_step, 0, unroll=4)
    lane = lax.broadcasted_iota(i32, (pairs, LANE), 1)
    chosen = jnp.zeros((pairs, LANE), i32)
    for q in range(4):
        word = words[q]
        for shift in (64, 32, 16, 8, 4, 2, 1):
            word = word | pltpu.roll(word, shift, 1)
        chosen = jnp.where((lane >> 5) == q, word, chosen)
    present = (jnp.right_shift(chosen, lane & 31) & 1).astype(f32).astype(bf16)
    tri = (
        lax.broadcasted_iota(i32, (LANE, LANE), 0) <= lax.broadcasted_iota(i32, (LANE, LANE), 1)
    ).astype(f32).astype(bf16)
    upto = jnp.dot(present, tri, preferred_element_type=f32).astype(i32)
    for s in range(pairs // 8):
        count = upto[8 * s : 8 * s + 8]
        slot = lane[0:8]
        found = jnp.zeros((8, LANE), i32)
        for step in (64, 32, 16, 8, 4, 2, 1):
            there = take_lanes(count, found + (step - 1))
            found = jnp.where(there <= slot, found + step, found)
        total = take_lanes(count, jnp.full((8, LANE), LANE - 1, i32))
        lists_ref[8 * s : 8 * s + 8, :] = found
        lists_ref[pairs + 8 * s : pairs + 8 * s + 8, :] = total

    for step in range(1, n):
        copy_to(step).wait()
    bounds_ref[...] = jnp.max(theirs[...], axis=0)
    keep.wait()
    wait()


def apply_into(out_ref, table_ref, lists_ref, ext_ref, vals_ref, cols_ref):
    unit = pack(ext_ref, table_ref)
    upper = lax.broadcasted_iota(i32, (8, LANE), 0) < 4

    def group_step(g, carry):
        base = g * PAIRS
        index = [pair_index(cols_ref, base + u) for u in range(PAIRS)]
        pairs = cols_ref.shape[1] // (2 * LANE)
        most = lists_ref[pairs + base, 0]
        for u in range(1, PAIRS):
            most = jnp.maximum(most, lists_ref[pairs + base + u, 0])
        chunks = (most + (CHUNK - 1)) // CHUNK

        def chunk_step(k, flat):
            flat = list(flat)
            for u in range(PAIRS):
                wanted = [lists_ref[base + u, k * CHUNK + t] for t in range(CHUNK)]
                flat[6 * u : 6 * u + 6] = visit_pair(
                    table_ref, wanted, *index[u], upper, flat[6 * u : 6 * u + 6]
                )
            return tuple(flat)

        zero = jnp.zeros((8, LANE), i32)
        flat = chunk_step(0, (zero,) * (6 * PAIRS))
        flat = lax.fori_loop(1, chunks, chunk_step, flat)
        for u in range(PAIRS):
            parts = [unpack((flat[6 * u + h], flat[6 * u + 3 + h])) for h in range(3)]
            for v in range(2):
                at = at_block(2 * (base + u) + v)
                gathered = [
                    jnp.concatenate([parts[v][j], parts[2][j][4 * v : 4 * v + 4]], axis=0)
                    for j in range(3)
                ]
                for c, row in enumerate(contract(vals_ref, at, gathered)):
                    out_ref[c : c + 1, at] = row
        return carry

    lax.fori_loop(0, cols_ref.shape[1] // (2 * LANE * PAIRS), group_step, 0)
    return unit


def apply_start(lists_ref, ext_ref, vals_ref, cols_ref, rhs_ref, dinv_ref, bounds_ref,
                res_ref, first_ref, scratch, table):
    unit = apply_into(scratch, table, lists_ref, ext_ref, vals_ref, cols_ref)
    theta = coefficients(bounds_ref[0:1, 0:1])[0]
    res = rhs_ref[...] - unit * scratch[...]
    res_ref[...] = res
    first_ref[...] = dinv_ref[...] * res / theta


def apply_first(lists_ref, ext_ref, vals_ref, cols_ref, res_ref, dinv_ref, bounds_ref, first_ref,
                start_ref, res_out, second_ref, iterate_ref, scratch, table):
    unit = apply_into(scratch, table, lists_ref, ext_ref, vals_ref, cols_ref)
    theta, delta, rho_zero, rho_one = coefficients(bounds_ref[0:1, 0:1])
    res = res_ref[...] - unit * scratch[...]
    res_out[...] = res
    first = first_ref[...]
    second = (rho_one * rho_zero) * first + (2.0 * rho_one / delta) * dinv_ref[...] * res
    second_ref[...] = second
    iterate_ref[...] = start_ref[...] + first + second


def apply_second(lists_ref, ext_ref, vals_ref, cols_ref, res_ref, prol_ref, place_ref,
                 sums_ref, scratch, table):
    unit = apply_into(scratch, table, lists_ref, ext_ref, vals_ref, cols_ref)
    count = scratch.shape[1]
    tiles = sums_ref.shape[1] // LANE
    piece = 8 * LANE
    offset = lax.axis_index("row") * (sums_ref.shape[1] - 2 * LANE) - LANE

    def step(p, acc):
        at = pl.ds(pl.multiple_of(p * piece, piece), piece)
        res = res_ref[:, at] - unit * scratch[:, at]
        contrib = jnp.zeros((3, piece), f32)
        for c in range(3):
            contrib = contrib + prol_ref[c, :, at].astype(f32) * res[c : c + 1]
        head = contrib.astype(bf16).astype(f32)
        tail = contrib - head
        both = jnp.concatenate([head, tail, jnp.zeros((2, piece), f32)], axis=0)
        place = place_ref[:, at] - offset
        high = jnp.broadcast_to(place >> 7, (8, piece))
        rows = jnp.concatenate([jnp.where(high == h, both, 0.0) for h in range(tiles)], axis=0)
        hot = jnp.where(
            jnp.broadcast_to(place & (LANE - 1), (LANE, piece))
            == lax.broadcasted_iota(i32, (LANE, piece), 0),
            1.0,
            0.0,
        ).astype(bf16)
        return acc + lax.dot_general(
            rows.astype(bf16), hot, (((1,), (1,)), ((), ())), preferred_element_type=f32
        )

    acc = lax.fori_loop(0, count // piece, step, jnp.zeros((8 * tiles, LANE), f32))
    for h in range(tiles):
        part = acc[8 * h : 8 * h + 8]
        sums_ref[:, h * LANE : (h + 1) * LANE] = part[0:3] + part[3:6]


def apply_coarse(table, vals_ref, cols_ref, out_ref):
    blocks = cols_ref.shape[1] // LANE
    for b in range(blocks):
        lanes, rows = halves(cols_ref[:, at_block(b)])
        acc = [jnp.zeros((8, LANE), f32)] * 6
        for r in range(2 * blocks):
            acc = visit(table, r, lanes, rows, acc)
        gathered = [jnp.concatenate([acc[2 * j], acc[2 * j + 1][0:4]], axis=0) for j in range(3)]
        for c, row in enumerate(contract(vals_ref, at_block(b), gathered)):
            out_ref[c : c + 1, at_block(b)] = row


def coarse_kernel(n, sums_ref, vals_ref, cols_ref, dinv_ref, bounds_ref,
                  t2, first_ref, res_ref, ghosts, d1, d2, t1, sends, recvs):
    me = lax.axis_index("row")
    own = dinv_ref.shape[1]
    blocks = own // LANE
    width = own // 2
    greet(me, n, False)
    wide = own + 2 * LANE
    low = pltpu.make_async_remote_copy(
        src_ref=sums_ref.at[:, pl.ds(0, LANE)], dst_ref=ghosts.at[1],
        send_sem=sends.at[0], recv_sem=recvs.at[0],
        device_id={"row": jnp.maximum(me - 1, 0)}, device_id_type=pl.DeviceIdType.MESH,
    )
    high = pltpu.make_async_remote_copy(
        src_ref=sums_ref.at[:, pl.ds(wide - LANE, LANE)], dst_ref=ghosts.at[0],
        send_sem=sends.at[1], recv_sem=recvs.at[1],
        device_id={"row": jnp.minimum(me + 1, n - 1)}, device_id_type=pl.DeviceIdType.MESH,
    )
    zeros = jnp.zeros((3, LANE), f32)

    @pl.when(me > 0)
    def _():
        low.start()

    @pl.when(me < n - 1)
    def _():
        high.start()

    @pl.when(me == 0)
    def _():
        ghosts[0] = zeros

    @pl.when(me == n - 1)
    def _():
        ghosts[1] = zeros

    theta, delta, rho_zero, rho_one = coefficients(bounds_ref[4:5, 0:1])
    dinv = dinv_ref[...]

    @pl.when(me > 0)
    def _():
        low.wait_send()
        high.wait_recv()

    @pl.when(me < n - 1)
    def _():
        high.wait_send()
        low.wait_recv()

    tiles = [sums_ref[:, (h + 1) * LANE : (h + 2) * LANE] for h in range(blocks)]
    tiles[0] = tiles[0] + ghosts[0]
    tiles[-1] = tiles[-1] + ghosts[1]
    res = jnp.concatenate(tiles, axis=1)

    def swap(value, held, table, k):
        held[...] = value
        start, wait = exchange(
            held, table, width, own, me, n, sends.at[pl.ds(2 * k, 2)], recvs.at[pl.ds(2 * k, 2)]
        )
        start()
        table[:, pl.ds(width, own)] = value
        wait()

    first = dinv * res / theta
    swap(first, d1, t1, 1)
    first_ref[...] = first
    apply_coarse(t1, vals_ref, cols_ref, res_ref)
    res = res - res_ref[...]
    res_ref[...] = res
    second = (rho_one * rho_zero) * first + (2.0 * rho_one / delta) * dinv * res
    swap(second, d2, t2, 2)


def coarse_last(t2, vals_ref, cols_ref, first_ref, res_ref, iterate_ref, out_ref):
    own = first_ref.shape[1]
    iterate_ref[...] = first_ref[...] + t2[:, own // 2 : own // 2 + own]
    apply_coarse(t2, vals_ref, cols_ref, out_ref)
    out_ref[...] = res_ref[...] - out_ref[...]


def params(collective=None, limit=24 * 1024 * 1024):
    if collective is None:
        return pltpu.CompilerParams(vmem_limit_bytes=limit)
    return pltpu.CompilerParams(
        vmem_limit_bytes=limit, collective_id=collective, has_side_effects=True
    )


def halo_kernel(n, vector_ref, ext_ref, sends, recvs, own_sem):
    me = lax.axis_index("row")
    own = vector_ref.shape[1]
    width = (ext_ref.shape[1] - own) // 2
    greet(me, n, False)
    start, wait = exchange(vector_ref, ext_ref, width, own, me, n, sends, recvs)
    start()
    keep = pltpu.make_async_copy(vector_ref, ext_ref.at[:, pl.ds(width, own)], own_sem)
    keep.start()
    keep.wait()
    wait()


def shards(n, start, rhs, fine_vals, fine_cols, prol, aggregate, coarse_vals, coarse_cols):
    nf, nc = start.shape[1], coarse_vals.shape[3]
    blocks = nf // LANE
    shape = jax.ShapeDtypeStruct
    fine, ext = shape((3, nf), f32), shape((3, 2 * nf), f32)
    coarse = shape((3, nc), f32)
    dma = pltpu.SemaphoreType.DMA

    ext0, lists, dinv, cdinv, bounds, vals, cols, cvals = pl.pallas_call(
        functools.partial(first_kernel, n),
        out_shape=(
            ext, shape((blocks, LANE), i32), fine, coarse, shape((8, LANE), f32),
            shape(fine_vals.shape, bf16), shape(fine_cols.shape, i32),
            shape(coarse_vals.shape, bf16),
        ),
        in_specs=[HBM] * 4,
        out_specs=(VMEM,) * 8,
        scratch_shapes=[
            pltpu.VMEM((4, blocks // 2, LANE), i32),
            pltpu.VMEM((8, LANE), f32),
            pltpu.VMEM((n, 8, LANE), f32),
            dma((2,)), dma((2,)), dma((n,)), dma((n,)), dma((7,)),
        ],
        compiler_params=params(0, 52_000_000),
        name="prepare",
    )(start, fine_vals, fine_cols, coarse_vals)

    def halo(vector, collective):
        return pl.pallas_call(
            functools.partial(halo_kernel, n),
            out_shape=ext,
            in_specs=[VMEM],
            out_specs=VMEM,
            scratch_shapes=[dma((2,)), dma((2,)), dma],
            compiler_params=params(collective),
            name=f"halo{collective}",
        )(vector)

    def applied(kernel, outs, *args):
        return pl.pallas_call(
            kernel,
            out_shape=outs,
            in_specs=[SMEM] + [VMEM] * len(args),
            out_specs=(VMEM,) * len(outs),
            scratch_shapes=[pltpu.VMEM((3, nf), f32), pltpu.VMEM((2, 2 * nf + LANE), i32)],
            compiler_params=params(),
            name=kernel.__name__,
        )(lists, *args)

    res, first = applied(
        apply_start, (fine, fine), ext0, vals, cols, rhs, dinv, bounds
    )
    res, second, iterate = applied(
        apply_first, (fine, fine, fine), halo(first, 1), vals, cols, res, dinv, bounds,
        first, start,
    )
    place = aggregate.reshape(1, nf)
    (sums,) = applied(
        apply_second, (shape((3, nc + 2 * LANE), f32),), halo(second, 2), vals, cols, res,
        prol, place,
    )
    table, first, res = pl.pallas_call(
        functools.partial(coarse_kernel, n),
        out_shape=(shape((3, 2 * nc), f32), coarse, coarse),
        in_specs=[VMEM] * 5,
        out_specs=(VMEM,) * 3,
        scratch_shapes=[
            pltpu.VMEM((2, 3, LANE), f32),
            pltpu.VMEM((3, nc), f32), pltpu.VMEM((3, nc), f32),
            pltpu.VMEM((3, 2 * nc), f32),
            dma((6,)), dma((6,)),
        ],
        compiler_params=params(3),
        name="coarse",
    )(sums, cvals, coarse_cols, cdinv, bounds)
    coarse_iterate, coarse_residual = pl.pallas_call(
        coarse_last,
        out_shape=(coarse, coarse),
        in_specs=[VMEM] * 5,
        out_specs=(VMEM,) * 2,
        compiler_params=params(),
        name="coarse_last",
    )(table, cvals, coarse_cols, first, res)
    return (iterate, coarse_iterate, coarse_residual)


def solution(mesh):
    in_specs = (
        P(None, ("grp", "row")),
        P(None, ("grp", "row")),
        P(None, None, None, ("grp", "row")),
        P(None, ("grp", "row")),
        P(None, None, ("grp", "row")),
        P(("grp", "row")),
        P(None, None, None, ("grp", "row")),
        P(None, ("grp", "row")),
    )
    out_specs = (P(None, ("grp", "row")), P(None, ("grp", "row")), P(None, ("grp", "row")))
    return jax.shard_map(
        functools.partial(shards, mesh.shape["row"]),
        mesh=mesh, in_specs=in_specs, out_specs=out_specs, check_vma=False,
    )
```

```python
import functools

import jax
import jax.numpy as jnp
from jax import lax
from jax.experimental import pallas as pl
from jax.experimental.pallas import tpu as pltpu
from jax.sharding import PartitionSpec as P

LANE = 128
CHUNK = 15
PAIRS = 4
STEPS = float(2**20 - 1)
lower_fraction = 0.1

f32, i32, bf16 = jnp.float32, jnp.int32, jnp.bfloat16
VMEM = pl.BlockSpec(memory_space=pltpu.VMEM)
SMEM = pl.BlockSpec(memory_space=pltpu.SMEM)
HBM = pl.BlockSpec(memory_space=pltpu.HBM)


def coefficients(bound):
    lowest = lower_fraction * bound
    theta = (bound + lowest) / 2.0
    delta = (bound - lowest) / 2.0
    sigma = theta / delta
    rho_zero = 1.0 / sigma
    rho_one = 1.0 / (2.0 * sigma - rho_zero)
    return (theta, delta, rho_zero, rho_one)


def at_block(b):
    if isinstance(b, int):
        return pl.ds(b * LANE, LANE)
    return pl.ds(pl.multiple_of(b * LANE, LANE), LANE)


def take_lanes(row, lanes):
    return jnp.take_along_axis(row, lanes, axis=1, mode="promise_in_bounds")


def pad_rows(x):
    return x[0:8], jnp.concatenate([x[8:12], x[8:12]], axis=0)


def halves(cols):
    parts = pad_rows(cols)
    return [p & (LANE - 1) for p in parts], [p >> 7 for p in parts]


def pair_index(cols_ref, p):
    cols = [cols_ref[:, at_block(2 * p + u)] for u in range(2)]
    rel = [((c >> 7) - u) & (LANE - 1) for u, c in enumerate(cols)]
    lanes = [c & (LANE - 1) for c in cols]
    return [
        (x[0][0:8], x[1][0:8], jnp.concatenate([x[0][8:12], x[1][8:12]], axis=0))
        for x in (lanes, rel)
    ]


def visit_pair(table_ref, wanted, lanes, rows, upper, acc):
    acc = list(acc)
    for h in range(3):
        for r in wanted:
            mask = rows[h] == r
            for w in range(2):
                two = table_ref[w : w + 1, pl.ds(pl.multiple_of(r * LANE, LANE), 2 * LANE)]
                first = jnp.broadcast_to(two[:, :LANE], (8, LANE))
                second = jnp.broadcast_to(two[:, LANE:], (8, LANE))
                src = (first, second, None)[h]
                if src is None:
                    src = jnp.where(upper, first, second)
                acc[3 * w + h] = jnp.where(mask, take_lanes(src, lanes[h]), acc[3 * w + h])
    return acc


def pack(ext_ref, table_ref):
    size = ext_ref.shape[1]
    piece = 16 * LANE

    def at(p):
        return pl.ds(pl.multiple_of(p * piece, piece), piece)

    def largest(p, most):
        return jnp.maximum(most, jnp.abs(ext_ref[:, at(p)]))

    most = lax.fori_loop(0, size // piece, largest, jnp.zeros((3, piece), f32))
    most = jnp.max(jnp.max(most, axis=1, keepdims=True), axis=0, keepdims=True)
    most = jnp.maximum(most, 1e-30)
    scale = STEPS / most

    def words(vector):
        fixed = jnp.round(vector * scale).astype(i32)
        third = jnp.broadcast_to(fixed[2:3] + 2**20, (2, vector.shape[1]))
        head = lax.broadcasted_iota(i32, third.shape, 0) == 0
        return jnp.left_shift(fixed[0:2], 11) | jnp.where(head, third >> 10, third & 1023)

    def step(p, carry):
        table_ref[:, at(p)] = words(ext_ref[:, at(p)])
        return carry

    lax.fori_loop(0, size // piece, step, 0)
    table_ref[:, size : size + LANE] = table_ref[:, 0:LANE]
    return most / STEPS


def unpack(words):
    one, two = words
    third = (jnp.left_shift(one & 2047, 10) | (two & 1023)) - 2**20
    return [x.astype(f32) for x in (one >> 11, two >> 11, third)]


def visit(table_ref, r, lanes, rows, acc):
    at = at_block(r)
    masks = [row == r for row in rows]
    out = []
    for j in range(3):
        src = jnp.broadcast_to(table_ref[j : j + 1, at], (8, LANE))
        for h in range(2):
            out.append(jnp.where(masks[h], take_lanes(src, lanes[h]), acc[2 * j + h]))
    return out


def contract(vals_ref, at, gathered):
    out = []
    for c in range(3):
        total = None
        for j in range(3):
            term = vals_ref[c, j, :, at].astype(f32) * gathered[j]
            total = term if total is None else total + term
        out.append(jnp.sum(total, axis=0, keepdims=True))
    return out


def bound_of_block(vals_ref, at, dinv_ref, best):
    for c in range(3):
        total = None
        for j in range(3):
            term = jnp.abs(vals_ref[c, j, :, at].astype(f32))
            total = term if total is None else total + term
        inverse = 1.0 / vals_ref[c, c, :, at].astype(f32)[0:1]
        dinv_ref[c : c + 1, at] = inverse
        best = jnp.maximum(best, jnp.sum(total, axis=0, keepdims=True) * inverse)
    return best


def neighbours(me, n):
    return ((me > 0, me - 1), (me < n - 1, me + 1))


def exchange(source, target, width, own, me, n, sends, recvs):
    low = pltpu.make_async_remote_copy(
        src_ref=source.at[:, pl.ds(0, width)],
        dst_ref=target.at[:, pl.ds(width + own, width)],
        send_sem=sends.at[0],
        recv_sem=recvs.at[0],
        device_id={"row": jnp.maximum(me - 1, 0)},
        device_id_type=pl.DeviceIdType.MESH,
    )
    high = pltpu.make_async_remote_copy(
        src_ref=source.at[:, pl.ds(own - width, width)],
        dst_ref=target.at[:, pl.ds(0, width)],
        send_sem=sends.at[1],
        recv_sem=recvs.at[1],
        device_id={"row": jnp.minimum(me + 1, n - 1)},
        device_id_type=pl.DeviceIdType.MESH,
    )

    def start():
        @pl.when(me > 0)
        def _():
            low.start()

        @pl.when(me < n - 1)
        def _():
            high.start()

        zeros = jnp.zeros((3, width), f32)

        @pl.when(me == 0)
        def _():
            target[:, pl.ds(0, width)] = zeros

        @pl.when(me == n - 1)
        def _():
            target[:, pl.ds(width + own, width)] = zeros

    def wait():
        @pl.when(me > 0)
        def _():
            low.wait_send()
            high.wait_recv()

        @pl.when(me < n - 1)
        def _():
            high.wait_send()
            low.wait_recv()

    return start, wait


def greet(me, n, everyone, between=lambda: None):
    barrier = pltpu.get_barrier_semaphore()
    if everyone:
        def one(step, carry):
            pl.semaphore_signal(
                barrier, inc=1, device_id={"row": lax.rem(me + step, n)},
                device_id_type=pl.DeviceIdType.MESH,
            )
            return carry

        lax.fori_loop(1, n, one, 0)
        between()
        pl.semaphore_wait(barrier, n - 1)
    else:
        for cond, who in neighbours(me, n):
            @pl.when(cond)
            def _():
                pl.semaphore_signal(
                    barrier, inc=1, device_id={"row": who}, device_id_type=pl.DeviceIdType.MESH
                )
        between()
        pl.semaphore_wait(barrier, jnp.minimum(me, 1) + jnp.minimum(n - 1 - me, 1))


def first_kernel(n, start_hbm, vals_hbm, cols_hbm, cvals_hbm,
                 ext_ref, lists_ref, dinv_ref, cdinv_ref, bounds_ref,
                 vals_ref, cols_ref, cvals_ref, words, mine, theirs,
                 sends, recvs, bsends, brecvs, local):
    me = lax.axis_index("row")
    own = start_hbm.shape[1]
    width = (ext_ref.shape[1] - own) // 2
    blocks, cblocks = own // LANE, cvals_ref.shape[3] // LANE
    part = own // 4
    fetch_vals = [
        pltpu.make_async_copy(
            vals_hbm.at[:, :, :, pl.ds(p * part, part)],
            vals_ref.at[:, :, :, pl.ds(p * part, part)],
            local.at[p],
        )
        for p in range(4)
    ]
    fetch_cvals = pltpu.make_async_copy(cvals_hbm, cvals_ref, local.at[4])
    fetch_cols = pltpu.make_async_copy(cols_hbm, cols_ref, local.at[5])
    keep = pltpu.make_async_copy(start_hbm, ext_ref.at[:, pl.ds(width, own)], local.at[6])
    for copy in (*fetch_vals, fetch_cvals, fetch_cols, keep):
        copy.start()
    start, wait = exchange(start_hbm, ext_ref, width, own, me, n, sends, recvs)

    def bounds():
        low = jnp.full((1, LANE), -jnp.inf, f32)

        def bound_step(g, best):
            for u in range(4):
                best = bound_of_block(vals_ref, at_block(g * 4 + u), dinv_ref, best)
            return best

        best = low
        for p in range(4):
            fetch_vals[p].wait()
            best = lax.fori_loop(p * (blocks // 16), (p + 1) * (blocks // 16), bound_step, best)
        fetch_cvals.wait()
        cbest = low
        for b in range(cblocks):
            cbest = bound_of_block(cvals_ref, at_block(b), cdinv_ref, cbest)
        both = jnp.concatenate([jnp.broadcast_to(x, (4, LANE)) for x in (best, cbest)], axis=0)
        for shift in (64, 32, 16, 8, 4, 2, 1):
            both = jnp.maximum(both, pltpu.roll(both, shift, 1))
        mine[...] = both
        theirs[0] = both

    greet(me, n, True, bounds)
    start()

    def copy_to(step):
        return pltpu.make_async_remote_copy(
            src_ref=mine,
            dst_ref=theirs.at[step],
            send_sem=bsends.at[step],
            recv_sem=brecvs.at[step],
            device_id={"row": lax.rem(me + step, n)},
            device_id_type=pl.DeviceIdType.MESH,
        )

    for step in range(1, n):
        copy_to(step).start()

    fetch_cols.wait()
    pairs = blocks // 2

    def word_step(p, carry):
        _, rows = pair_index(cols_ref, p)
        bits = [jnp.left_shift(1, row & 31) for row in rows]
        for q in range(4):
            word = functools.reduce(
                jnp.bitwise_or, [jnp.where((rows[h] >> 5) == q, bits[h], 0) for h in range(3)]
            )
            word = word[0:4] | word[4:8]
            word = word[0:2] | word[2:4]
            words[q, pl.ds(p, 1), :] = word[0:1] | word[1:2]
        return carry

    lax.fori_loop(0, pairs, word_step, 0, unroll=4)
    lane = lax.broadcasted_iota(i32, (pairs, LANE), 1)
    chosen = jnp.zeros((pairs, LANE), i32)
    for q in range(4):
        word = words[q]
        for shift in (64, 32, 16, 8, 4, 2, 1):
            word = word | pltpu.roll(word, shift, 1)
        chosen = jnp.where((lane >> 5) == q, word, chosen)
    present = (jnp.right_shift(chosen, lane & 31) & 1).astype(f32).astype(bf16)
    tri = (
        lax.broadcasted_iota(i32, (LANE, LANE), 0) <= lax.broadcasted_iota(i32, (LANE, LANE), 1)
    ).astype(f32).astype(bf16)
    upto = jnp.dot(present, tri, preferred_element_type=f32).astype(i32)
    for s in range(pairs // 8):
        count = upto[8 * s : 8 * s + 8]
        slot = lane[0:8]
        found = jnp.zeros((8, LANE), i32)
        for step in (64, 32, 16, 8, 4, 2, 1):
            there = take_lanes(count, found + (step - 1))
            found = jnp.where(there <= slot, found + step, found)
        total = take_lanes(count, jnp.full((8, LANE), LANE - 1, i32))
        lists_ref[8 * s : 8 * s + 8, :] = found
        lists_ref[pairs + 8 * s : pairs + 8 * s + 8, :] = total

    for step in range(1, n):
        copy_to(step).wait()
    bounds_ref[...] = jnp.max(theirs[...], axis=0)
    keep.wait()
    wait()


def apply_into(out_ref, table_ref, lists_ref, ext_ref, vals_ref, cols_ref):
    unit = pack(ext_ref, table_ref)
    upper = lax.broadcasted_iota(i32, (8, LANE), 0) < 4

    def group_step(g, carry):
        base = g * PAIRS
        index = [pair_index(cols_ref, base + u) for u in range(PAIRS)]
        pairs = cols_ref.shape[1] // (2 * LANE)
        most = lists_ref[pairs + base, 0]
        for u in range(1, PAIRS):
            most = jnp.maximum(most, lists_ref[pairs + base + u, 0])
        chunks = (most + (CHUNK - 1)) // CHUNK

        def chunk_step(k, flat):
            flat = list(flat)
            for u in range(PAIRS):
                wanted = [
                    lists_ref[base + u, t if isinstance(k, int) else jnp.minimum(k * CHUNK + t, LANE - 1)]
                    for t in range(CHUNK)
                ]
                flat[6 * u : 6 * u + 6] = visit_pair(
                    table_ref, wanted, *index[u], upper, flat[6 * u : 6 * u + 6]
                )
            return tuple(flat)

        zero = jnp.zeros((8, LANE), i32)
        flat = chunk_step(0, (zero,) * (6 * PAIRS))
        flat = lax.fori_loop(1, chunks, chunk_step, flat)
        for u in range(PAIRS):
            parts = [unpack((flat[6 * u + h], flat[6 * u + 3 + h])) for h in range(3)]
            for v in range(2):
                at = at_block(2 * (base + u) + v)
                gathered = [
                    jnp.concatenate([parts[v][j], parts[2][j][4 * v : 4 * v + 4]], axis=0)
                    for j in range(3)
                ]
                for c, row in enumerate(contract(vals_ref, at, gathered)):
                    out_ref[c : c + 1, at] = row
        return carry

    lax.fori_loop(0, cols_ref.shape[1] // (2 * LANE * PAIRS), group_step, 0)
    return unit


def apply_start(lists_ref, ext_ref, vals_ref, cols_ref, rhs_ref, dinv_ref, bounds_ref,
                res_ref, first_ref, scratch, table):
    unit = apply_into(scratch, table, lists_ref, ext_ref, vals_ref, cols_ref)
    theta = coefficients(bounds_ref[0:1, 0:1])[0]
    res = rhs_ref[...] - unit * scratch[...]
    res_ref[...] = res
    first_ref[...] = dinv_ref[...] * res / theta


def apply_first(lists_ref, ext_ref, vals_ref, cols_ref, res_ref, dinv_ref, bounds_ref, first_ref,
                start_ref, res_out, second_ref, iterate_ref, scratch, table):
    unit = apply_into(scratch, table, lists_ref, ext_ref, vals_ref, cols_ref)
    theta, delta, rho_zero, rho_one = coefficients(bounds_ref[0:1, 0:1])
    res = res_ref[...] - unit * scratch[...]
    res_out[...] = res
    first = first_ref[...]
    second = (rho_one * rho_zero) * first + (2.0 * rho_one / delta) * dinv_ref[...] * res
    second_ref[...] = second
    iterate_ref[...] = start_ref[...] + first + second


def apply_second(lists_ref, ext_ref, vals_ref, cols_ref, res_ref, prol_ref, place_ref,
                 sums_ref, scratch, table):
    unit = apply_into(scratch, table, lists_ref, ext_ref, vals_ref, cols_ref)
    count = scratch.shape[1]
    tiles = sums_ref.shape[1] // LANE
    piece = 8 * LANE
    offset = lax.axis_index("row") * (sums_ref.shape[1] - 2 * LANE) - LANE

    def step(p, acc):
        at = pl.ds(pl.multiple_of(p * piece, piece), piece)
        res = res_ref[:, at] - unit * scratch[:, at]
        contrib = jnp.zeros((3, piece), f32)
        for c in range(3):
            contrib = contrib + prol_ref[c, :, at].astype(f32) * res[c : c + 1]
        head = contrib.astype(bf16).astype(f32)
        tail = contrib - head
        both = jnp.concatenate([head, tail, jnp.zeros((2, piece), f32)], axis=0)
        place = place_ref[:, at] - offset
        high = jnp.broadcast_to(place >> 7, (8, piece))
        rows = jnp.concatenate([jnp.where(high == h, both, 0.0) for h in range(tiles)], axis=0)
        hot = jnp.where(
            jnp.broadcast_to(place & (LANE - 1), (LANE, piece))
            == lax.broadcasted_iota(i32, (LANE, piece), 0),
            1.0,
            0.0,
        ).astype(bf16)
        return acc + lax.dot_general(
            rows.astype(bf16), hot, (((1,), (1,)), ((), ())), preferred_element_type=f32
        )

    acc = lax.fori_loop(0, count // piece, step, jnp.zeros((8 * tiles, LANE), f32))
    for h in range(tiles):
        part = acc[8 * h : 8 * h + 8]
        sums_ref[:, h * LANE : (h + 1) * LANE] = part[0:3] + part[3:6]


def apply_coarse(table, vals_ref, cols_ref, out_ref):
    blocks = cols_ref.shape[1] // LANE
    for b in range(blocks):
        lanes, rows = halves(cols_ref[:, at_block(b)])
        acc = [jnp.zeros((8, LANE), f32)] * 6
        for r in range(2 * blocks):
            acc = visit(table, r, lanes, rows, acc)
        gathered = [jnp.concatenate([acc[2 * j], acc[2 * j + 1][0:4]], axis=0) for j in range(3)]
        for c, row in enumerate(contract(vals_ref, at_block(b), gathered)):
            out_ref[c : c + 1, at_block(b)] = row


def coarse_kernel(n, sums_ref, vals_ref, cols_ref, dinv_ref, bounds_ref,
                  t2, first_ref, res_ref, ghosts, d1, d2, t1, sends, recvs):
    me = lax.axis_index("row")
    own = dinv_ref.shape[1]
    blocks = own // LANE
    width = own // 2
    greet(me, n, False)
    wide = own + 2 * LANE
    low = pltpu.make_async_remote_copy(
        src_ref=sums_ref.at[:, pl.ds(0, LANE)], dst_ref=ghosts.at[1],
        send_sem=sends.at[0], recv_sem=recvs.at[0],
        device_id={"row": jnp.maximum(me - 1, 0)}, device_id_type=pl.DeviceIdType.MESH,
    )
    high = pltpu.make_async_remote_copy(
        src_ref=sums_ref.at[:, pl.ds(wide - LANE, LANE)], dst_ref=ghosts.at[0],
        send_sem=sends.at[1], recv_sem=recvs.at[1],
        device_id={"row": jnp.minimum(me + 1, n - 1)}, device_id_type=pl.DeviceIdType.MESH,
    )
    zeros = jnp.zeros((3, LANE), f32)

    @pl.when(me > 0)
    def _():
        low.start()

    @pl.when(me < n - 1)
    def _():
        high.start()

    @pl.when(me == 0)
    def _():
        ghosts[0] = zeros

    @pl.when(me == n - 1)
    def _():
        ghosts[1] = zeros

    theta, delta, rho_zero, rho_one = coefficients(bounds_ref[4:5, 0:1])
    dinv = dinv_ref[...]

    @pl.when(me > 0)
    def _():
        low.wait_send()
        high.wait_recv()

    @pl.when(me < n - 1)
    def _():
        high.wait_send()
        low.wait_recv()

    tiles = [sums_ref[:, (h + 1) * LANE : (h + 2) * LANE] for h in range(blocks)]
    tiles[0] = tiles[0] + ghosts[0]
    tiles[-1] = tiles[-1] + ghosts[1]
    res = jnp.concatenate(tiles, axis=1)

    def swap(value, held, table, k):
        held[...] = value
        start, wait = exchange(
            held, table, width, own, me, n, sends.at[pl.ds(2 * k, 2)], recvs.at[pl.ds(2 * k, 2)]
        )
        start()
        table[:, pl.ds(width, own)] = value
        wait()

    first = dinv * res / theta
    swap(first, d1, t1, 1)
    first_ref[...] = first
    apply_coarse(t1, vals_ref, cols_ref, res_ref)
    res = res - res_ref[...]
    res_ref[...] = res
    second = (rho_one * rho_zero) * first + (2.0 * rho_one / delta) * dinv * res
    swap(second, d2, t2, 2)


def coarse_last(t2, vals_ref, cols_ref, first_ref, res_ref, iterate_ref, out_ref):
    own = first_ref.shape[1]
    iterate_ref[...] = first_ref[...] + t2[:, own // 2 : own // 2 + own]
    apply_coarse(t2, vals_ref, cols_ref, out_ref)
    out_ref[...] = res_ref[...] - out_ref[...]


def params(collective=None, limit=24 * 1024 * 1024):
    if collective is None:
        return pltpu.CompilerParams(vmem_limit_bytes=limit)
    return pltpu.CompilerParams(
        vmem_limit_bytes=limit, collective_id=collective, has_side_effects=True
    )


def halo_kernel(n, vector_ref, ext_ref, sends, recvs, own_sem):
    me = lax.axis_index("row")
    own = vector_ref.shape[1]
    width = (ext_ref.shape[1] - own) // 2
    greet(me, n, False)
    start, wait = exchange(vector_ref, ext_ref, width, own, me, n, sends, recvs)
    start()
    keep = pltpu.make_async_copy(vector_ref, ext_ref.at[:, pl.ds(width, own)], own_sem)
    keep.start()
    keep.wait()
    wait()


def shards(n, start, rhs, fine_vals, fine_cols, prol, aggregate, coarse_vals, coarse_cols):
    nf, nc = start.shape[1], coarse_vals.shape[3]
    blocks = nf // LANE
    shape = jax.ShapeDtypeStruct
    fine, ext = shape((3, nf), f32), shape((3, 2 * nf), f32)
    coarse = shape((3, nc), f32)
    dma = pltpu.SemaphoreType.DMA

    ext0, lists, dinv, cdinv, bounds, vals, cols, cvals = pl.pallas_call(
        functools.partial(first_kernel, n),
        out_shape=(
            ext, shape((blocks, LANE), i32), fine, coarse, shape((8, LANE), f32),
            shape(fine_vals.shape, bf16), shape(fine_cols.shape, i32),
            shape(coarse_vals.shape, bf16),
        ),
        in_specs=[HBM] * 4,
        out_specs=(VMEM,) * 8,
        scratch_shapes=[
            pltpu.VMEM((4, blocks // 2, LANE), i32),
            pltpu.VMEM((8, LANE), f32),
            pltpu.VMEM((n, 8, LANE), f32),
            dma((2,)), dma((2,)), dma((n,)), dma((n,)), dma((7,)),
        ],
        compiler_params=params(0, 52_000_000),
        name="prepare",
    )(start, fine_vals, fine_cols, coarse_vals)

    def halo(vector, collective):
        return pl.pallas_call(
            functools.partial(halo_kernel, n),
            out_shape=ext,
            in_specs=[VMEM],
            out_specs=VMEM,
            scratch_shapes=[dma((2,)), dma((2,)), dma],
            compiler_params=params(collective),
            name=f"halo{collective}",
        )(vector)

    def applied(kernel, outs, *args):
        return pl.pallas_call(
            kernel,
            out_shape=outs,
            in_specs=[SMEM] + [VMEM] * len(args),
            out_specs=(VMEM,) * len(outs),
            scratch_shapes=[pltpu.VMEM((3, nf), f32), pltpu.VMEM((2, 2 * nf + LANE), i32)],
            compiler_params=params(),
            name=kernel.__name__,
        )(lists, *args)

    res, first = applied(
        apply_start, (fine, fine), ext0, vals, cols, rhs, dinv, bounds
    )
    res, second, iterate = applied(
        apply_first, (fine, fine, fine), halo(first, 1), vals, cols, res, dinv, bounds,
        first, start,
    )
    place = aggregate.reshape(1, nf)
    (sums,) = applied(
        apply_second, (shape((3, nc + 2 * LANE), f32),), halo(second, 2), vals, cols, res,
        prol, place,
    )
    table, first, res = pl.pallas_call(
        functools.partial(coarse_kernel, n),
        out_shape=(shape((3, 2 * nc), f32), coarse, coarse),
        in_specs=[VMEM] * 5,
        out_specs=(VMEM,) * 3,
        scratch_shapes=[
            pltpu.VMEM((2, 3, LANE), f32),
            pltpu.VMEM((3, nc), f32), pltpu.VMEM((3, nc), f32),
            pltpu.VMEM((3, 2 * nc), f32),
            dma((6,)), dma((6,)),
        ],
        compiler_params=params(3),
        name="coarse",
    )(sums, cvals, coarse_cols, cdinv, bounds)
    coarse_iterate, coarse_residual = pl.pallas_call(
        coarse_last,
        out_shape=(coarse, coarse),
        in_specs=[VMEM] * 5,
        out_specs=(VMEM,) * 2,
        compiler_params=params(),
        name="coarse_last",
    )(table, cvals, coarse_cols, first, res)
    return (iterate, coarse_iterate, coarse_residual)


def solution(mesh):
    in_specs = (
        P(None, ("grp", "row")),
        P(None, ("grp", "row")),
        P(None, None, None, ("grp", "row")),
        P(None, ("grp", "row")),
        P(None, None, ("grp", "row")),
        P(("grp", "row")),
        P(None, None, None, ("grp", "row")),
        P(None, ("grp", "row")),
    )
    out_specs = (P(None, ("grp", "row")), P(None, ("grp", "row")), P(None, ("grp", "row")))
    return jax.shard_map(
        functools.partial(shards, mesh.shape["row"]),
        mesh=mesh, in_specs=in_specs, out_specs=out_specs, check_vma=False,
    )
```
